32 devices in a mesh: rep: 8 (over y, x, core), grp: 4 (over z).
Axes of the slice: x: 2, y: 2, z: 4, core: 2. Of those that a mesh axis runs over, the one named last changes fastest.
Arguments:
- latents: bfloat16 [8, 1024, 1152], P('rep', 'grp'), may hold values from -6 to 6
- condition: bfloat16 [8, 1152], P('rep'), may hold values from -6 to 6
- cotangent: bfloat16 [8, 1024, 1152], P('rep', 'grp'), may hold values from -6 to 6
- ada_weight: bfloat16 [1152, 6912], P('grp'), may hold values from -0.1875 to 0.1875
- ada_bias: bfloat16 [6912], P('grp'), may hold values from -3 to 3
- qkv_weight: bfloat16 [1152, 3456], P('grp'), may hold values from -0.1875 to 0.1875
- qv_bias: bfloat16 [2304], P('grp'), may hold values from -3 to 3
- proj_weight: bfloat16 [1152, 1152], P('grp'), may hold values from -6 to 6
- proj_bias: bfloat16 [1152], P('grp'), may hold values from -3 to 3
- fc1_weight: bfloat16 [1152, 4608], P('grp'), may hold values from -0.1875 to 0.1875
- fc1_bias: bfloat16 [4608], P('grp'), may hold values from -3 to 3
- fc2_weight: bfloat16 [4608, 1152], P('grp'), may hold values from -0.09375 to 0.09375
- fc2_bias: bfloat16 [1152], P('grp'), may hold values from -3 to 3
Outputs:
- output: float32 [8, 1024, 1152], P('rep', 'grp')
- grad_latents: float32 [8, 1024, 1152], P('rep', 'grp')
- grad_condition: float32 [8, 1152], P('rep')
- grad_ada_weight: float32 [1152, 6912], P('grp')
- grad_ada_bias: float32 [6912], P('grp')
- grad_qkv_weight: float32 [1152, 3456], P('grp')
- grad_qv_bias: float32 [2304], P('grp')
- grad_proj_weight: float32 [1152, 1152], P('grp')
- grad_proj_bias: float32 [1152], P('grp')
- grad_fc1_weight: float32 [1152, 4608], P('grp')
- grad_fc1_bias: float32 [4608], P('grp')
- grad_fc2_weight: float32 [4608, 1152], P('grp')
- grad_fc2_bias: float32 [1152], P('grp')
The draws below stay inside these ranges and needn't reach their ends.
All inputs are finite; a program needn't handle non-finite values.
Results may differ from the reference program's by a relative error of at most 0.019.
Values may be sent and summed in bfloat16 or wider, within the bound.
No kernel may reach another device: no remote copies, remote signals or barrier semaphores. Data moves between devices by JAX's collectives and lax.ppermute only.
A program may use at most 320 MiB of HBM per device.

```python
import jax
import jax.numpy as jnp
from jax import lax

D = 1152
HEADS = 16
HDIM = 72
FF = 4608
SEQ = 1024
LATENTS = 8


def levels(own_key, dims, cuts, smallest, largest):
    loudness, own = 1.0, jax.random.fold_in(own_key, 6)
    for position, shards_of in cuts:
        heights = jnp.exp(jax.random.uniform(jax.random.fold_in(own, position), (shards_of,), jnp.float32, smallest / len(cuts), largest / len(cuts)))
        loudness = loudness * jnp.repeat(heights, dims[position] // shards_of).reshape([-1 if axis == position else 1 for axis in range(len(dims))])
    return loudness


def gaussian(stream_key, shape, spread, limit, pieces=(), kind=jnp.bfloat16):
    drawn = jax.random.normal(stream_key, shape, jnp.float32) * spread
    if len(pieces) > 0:
        drawn = levels(stream_key, shape, pieces, -0.22, 0.18) * drawn
    return jnp.clip(drawn, min=-limit, max=limit).astype(kind)


def setup_inputs(seed: int = 0) -> dict:
    seeds = jax.random.split(jax.random.key(seed), 14)
    return {
        "latents": gaussian(seeds[0], (LATENTS, SEQ, D), 1.0, 6.0, ((0, 8), (1, 4))),
        "condition": gaussian(seeds[1], (LATENTS, D), 1.0, 6.0, ((0, 8),)),
        "cotangent": gaussian(seeds[2], (LATENTS, SEQ, D), 1.0, 6.0, ((0, 8), (1, 4))),
        "ada_weight": gaussian(seeds[3], (D, 6 * D), D ** -0.5, 0.1875, ((0, 4),)),
        "ada_bias": gaussian(seeds[4], (6 * D,), 0.5, 3.0, ((0, 4),)),
        "qkv_weight": gaussian(seeds[5], (D, 3 * D), D ** -0.5, 0.1875, ((0, 4),)),
        "qv_bias": gaussian(seeds[6], (2 * D,), 0.5, 3.0, ((0, 4),)),
        "proj_weight": gaussian(seeds[7], (D, D), (max(D // SEQ, 1)) ** -0.5, 6.0, ((0, 4),)),
        "proj_bias": gaussian(seeds[8], (D,), 0.5, 3.0, ((0, 4),)),
        "fc1_weight": gaussian(seeds[9], (D, FF), D ** -0.5, 0.1875, ((0, 4),)),
        "fc1_bias": gaussian(seeds[10], (FF,), 0.5, 3.0, ((0, 4),)),
        "fc2_weight": gaussian(seeds[11], (FF, D), FF ** -0.5, 0.09375, ((0, 4),)),
        "fc2_bias": gaussian(seeds[12], (D,), 0.5, 3.0, ((0, 4),)),
    }


norm_eps = 1e-06

def layer_norm(values):
    centre = values - lax.optimization_barrier(jnp.mean(values, axis=-1, keepdims=True))
    inverse = lax.rsqrt(lax.optimization_barrier(jnp.mean(centre * centre, axis=-1, keepdims=True)) + norm_eps)
    return (centre * inverse, inverse)

def norm_back(normed, inverse, grad):
    return inverse * (grad - lax.optimization_barrier(jnp.mean(grad, axis=-1, keepdims=True)) - normed * lax.optimization_barrier(jnp.mean(grad * normed, axis=-1, keepdims=True)))

def silu_float(values):
    return values * jax.nn.sigmoid(values)

def gelu_float(values):
    return jax.nn.gelu(values, approximate=True)

def reference(latents, condition, cotangent, ada_weight, ada_bias, qkv_weight, qv_bias, proj_weight, proj_bias, fc1_weight, fc1_bias, fc2_weight, fc2_bias):
    score_scale = float(HDIM) ** (-0.5)
    cond_silu = silu_float(condition.astype(jnp.float32)).astype(jnp.bfloat16)
    modulation = jnp.dot(cond_silu, ada_weight, preferred_element_type=jnp.float32) + ada_bias.astype(jnp.float32)
    bias_query = qv_bias[:D].astype(jnp.float32)
    bias_value = qv_bias[D:].astype(jnp.float32)

    def one_latent(totals, inputs):
        block_in, block_grad, latent_mod = inputs
        shift1, scale1, gate1, shift2, scale2, gate2 = [latent_mod[section * D:(section + 1) * D] for section in range(6)]
        input_float = block_in.astype(jnp.float32)
        normed1, inverse1 = layer_norm(input_float)
        adapted1 = (normed1 * (1.0 + scale1) + shift1).astype(jnp.bfloat16)
        projected = jnp.dot(adapted1, qkv_weight, preferred_element_type=jnp.float32)
        queries = (projected[:, :D] + bias_query).astype(jnp.bfloat16)
        keys = projected[:, D:2 * D].astype(jnp.bfloat16)
        values = (projected[:, 2 * D:] + bias_value).astype(jnp.bfloat16)
        query_heads = queries.astype(jnp.float32).reshape(SEQ, HEADS, HDIM)
        key_heads = keys.astype(jnp.float32).reshape(SEQ, HEADS, HDIM)
        value_heads = values.astype(jnp.float32).reshape(SEQ, HEADS, HDIM)
        scores = jnp.einsum('qhd,khd->hqk', query_heads, key_heads) * score_scale
        row_top = lax.optimization_barrier(jnp.max(scores, axis=-1, keepdims=True))
        log_total = row_top + jnp.log(lax.optimization_barrier(jnp.sum(jnp.exp(scores - row_top), axis=-1, keepdims=True)))
        probs = jnp.exp(scores - log_total)
        probs_b = probs.astype(jnp.bfloat16)
        attended = jnp.einsum('hqk,khd->qhd', probs_b.astype(jnp.float32), value_heads).reshape(SEQ, D).astype(jnp.bfloat16)
        attn_out = jnp.dot(attended, proj_weight, preferred_element_type=jnp.float32) + proj_bias.astype(jnp.float32)
        middle = input_float + gate1 * attn_out
        normed2, inverse2 = layer_norm(middle)
        adapted2 = (normed2 * (1.0 + scale2) + shift2).astype(jnp.bfloat16)
        hidden = jnp.dot(adapted2, fc1_weight, preferred_element_type=jnp.float32) + fc1_bias.astype(jnp.float32)
        activated = gelu_float(hidden).astype(jnp.bfloat16)
        mlp_out = jnp.dot(activated, fc2_weight, preferred_element_type=jnp.float32) + fc2_bias.astype(jnp.float32)
        block_out = middle + gate2 * mlp_out
        grad_out = block_grad.astype(jnp.float32)
        d_gate2 = lax.optimization_barrier(jnp.sum(grad_out * mlp_out, axis=0))
        grad_m = grad_out * gate2
        grad_m_b = grad_m.astype(jnp.bfloat16)
        grad_fc2 = jnp.dot(activated.T, grad_m_b, preferred_element_type=jnp.float32)
        grad_act = jnp.dot(grad_m_b, fc2_weight.T, preferred_element_type=jnp.float32)
        grad_h = jax.vjp(gelu_float, hidden)[1](grad_act)[0]
        grad_h_b = grad_h.astype(jnp.bfloat16)
        grad_fc1 = jnp.dot(adapted2.T, grad_h_b, preferred_element_type=jnp.float32)
        grad_a2 = jnp.dot(grad_h_b, fc1_weight.T, preferred_element_type=jnp.float32)
        d_shift2 = lax.optimization_barrier(jnp.sum(grad_a2, axis=0))
        d_scale2 = lax.optimization_barrier(jnp.sum(grad_a2 * normed2, axis=0))
        grad_mid = grad_out + norm_back(normed2, inverse2, grad_a2 * (1.0 + scale2))
        d_gate1 = lax.optimization_barrier(jnp.sum(grad_mid * attn_out, axis=0))
        grad_att = grad_mid * gate1
        grad_att_b = grad_att.astype(jnp.bfloat16)
        grad_proj = jnp.dot(attended.T, grad_att_b, preferred_element_type=jnp.float32)
        grad_o = jnp.dot(grad_att_b, proj_weight.T, preferred_element_type=jnp.float32).astype(jnp.bfloat16)
        grad_o_heads = grad_o.astype(jnp.float32).reshape(SEQ, HEADS, HDIM)
        dprobs = jnp.einsum('qhd,khd->hqk', grad_o_heads, value_heads)
        delta = lax.optimization_barrier(jnp.sum(probs * dprobs, axis=-1, keepdims=True))
        dscores = (probs * (dprobs - delta)).astype(jnp.bfloat16).astype(jnp.float32)
        grad_q = jnp.einsum('hqk,khd->qhd', dscores, key_heads).reshape(SEQ, D) * score_scale
        grad_k = jnp.einsum('hqk,qhd->khd', dscores, query_heads).reshape(SEQ, D) * score_scale
        grad_v = jnp.einsum('hqk,qhd->khd', probs_b.astype(jnp.float32), grad_o_heads).reshape(SEQ, D)
        grad_qkv_b = jnp.concatenate([grad_q, grad_k, grad_v], axis=-1).astype(jnp.bfloat16)
        grad_qkv = jnp.dot(adapted1.T, grad_qkv_b, preferred_element_type=jnp.float32)
        grad_a1 = jnp.dot(grad_qkv_b, qkv_weight.T, preferred_element_type=jnp.float32)
        d_shift1 = lax.optimization_barrier(jnp.sum(grad_a1, axis=0))
        d_scale1 = lax.optimization_barrier(jnp.sum(grad_a1 * normed1, axis=0))
        grad_in = grad_mid + norm_back(normed1, inverse1, grad_a1 * (1.0 + scale1))
        grad_mod = jnp.concatenate([d_shift1, d_scale1, d_gate1, d_shift2, d_scale2, d_gate2])
        grad_qv = jnp.concatenate([lax.optimization_barrier(jnp.sum(grad_q, axis=0)), lax.optimization_barrier(jnp.sum(grad_v, axis=0))])
        terms = (grad_qkv, grad_qv, grad_proj, lax.optimization_barrier(jnp.sum(grad_att, axis=0)), grad_fc1, lax.optimization_barrier(jnp.sum(grad_h, axis=0)), grad_fc2, lax.optimization_barrier(jnp.sum(grad_m, axis=0)))
        totals = tuple((total + term for total, term in zip(totals, terms)))
        return (totals, (block_out, grad_in, grad_mod))
    start = (jnp.zeros((D, 3 * D), jnp.float32), jnp.zeros((2 * D,), jnp.float32), jnp.zeros((D, D), jnp.float32), jnp.zeros((D,), jnp.float32), jnp.zeros((D, FF), jnp.float32), jnp.zeros((FF,), jnp.float32), jnp.zeros((FF, D), jnp.float32), jnp.zeros((D,), jnp.float32))
    totals, stacked = lax.scan(one_latent, start, (latents, cotangent, modulation))
    output, grad_latents, grad_mod = stacked
    grad_ada_weight = jnp.dot(cond_silu.astype(jnp.float32).T, grad_mod, precision=lax.Precision.HIGHEST)
    grad_ada_bias = lax.optimization_barrier(jnp.sum(grad_mod, axis=0))
    grad_silu = jnp.dot(grad_mod, ada_weight.astype(jnp.float32).T, precision=lax.Precision.HIGHEST)
    grad_condition = jax.vjp(silu_float, condition.astype(jnp.float32))[1](grad_silu)[0]
    grad_qkv, grad_qv, grad_proj, grad_proj_b, grad_fc1, grad_fc1_b, grad_fc2, grad_fc2_b = totals
    return (output, grad_latents, grad_condition, grad_ada_weight, grad_ada_bias, grad_qkv, grad_qv, grad_proj, grad_proj_b, grad_fc1, grad_fc1_b, grad_fc2, grad_fc2_b)
```

```python
import functools
import math

import jax
import jax.numpy as jnp
from jax import lax
from jax.experimental import pallas as pl
from jax.experimental.pallas import tpu as pltpu
from jax.sharding import PartitionSpec as P

HEADS = 16
HDIM = 72
EPS = 1e-06
LOG2E = math.log2(math.e)
BF = jnp.bfloat16
F32 = jnp.float32
NT = (((1,), (1,)), ((), ()))
NN = (((1,), (0,)), ((), ()))
TN = (((0,), (0,)), ((), ()))


def dot(a, b, dims=NN):
    return lax.dot_general(a, b, dims, preferred_element_type=F32)


def parts_of(ref, rows, h):
    width = ref.shape[1] // 3
    return [ref[rows, k * width + h * HDIM : k * width + (h + 1) * HDIM] for k in range(3)]


def attend_kernel(heads, tile, x_ref, o_ref, lse_ref):
    factor = HDIM**-0.5 * LOG2E
    rows = pl.ds(pl.multiple_of(pl.program_id(0) * tile, tile), tile)
    for h in range(heads):
        queries = parts_of(x_ref, rows, h)[0]
        _, keys, values = parts_of(x_ref, slice(None), h)
        scores = dot(keys, queries, NT)
        top = jnp.max(scores, axis=0, keepdims=True)
        weights = jnp.exp2((scores - top) * factor)
        total = jnp.sum(weights, axis=0, keepdims=True)
        mixed = dot(values, weights.astype(BF), TN)
        o_ref[:, h * HDIM : (h + 1) * HDIM] = (mixed / total).T.astype(BF)
        lse_ref[h : h + 1, :] = top * factor + jnp.log2(total)


def attend(x, tile):
    seq, width = x.shape[0], x.shape[1] // 3
    heads = width // HDIM
    return pl.pallas_call(
        functools.partial(attend_kernel, heads, tile),
        grid=(seq // tile,),
        in_specs=[pl.BlockSpec((seq, 3 * width), lambda i: (0, 0))],
        out_specs=[
            pl.BlockSpec((tile, width), lambda i: (i, 0)),
            pl.BlockSpec((heads, tile), lambda i: (0, i)),
        ],
        out_shape=[
            jax.ShapeDtypeStruct((seq, width), BF),
            jax.ShapeDtypeStruct((heads, seq), F32),
        ],
        cost_estimate=pl.CostEstimate(
            flops=4 * seq * seq * width,
            bytes_accessed=8 * seq * width,
            transcendentals=heads * seq * seq,
        ),
        name="attend",
    )(x)


def attend_back_kernel(heads, tile, x_ref, g_ref, lse_ref, d_ref, sum_ref, dk_acc, dv_acc):
    step = pl.program_id(0)
    scale = HDIM**-0.5
    width = heads * HDIM
    rows = pl.ds(pl.multiple_of(step * tile, tile), tile)

    @pl.when(step == 0)
    def _():
        dk_acc[...] = jnp.zeros_like(dk_acc)
        dv_acc[...] = jnp.zeros_like(dv_acc)
        sum_ref[...] = jnp.zeros_like(sum_ref)

    for h in range(heads):
        cols = slice(h * HDIM, (h + 1) * HDIM)
        queries = parts_of(x_ref, rows, h)[0]
        _, keys, values = parts_of(x_ref, slice(None), h)
        grads = g_ref[:, cols]
        probs = jnp.exp2(dot(keys, queries, NT) * (scale * LOG2E) - lse_ref[h : h + 1, :])
        dprobs = dot(values, grads, NT)
        delta = jnp.sum(probs * dprobs, axis=0, keepdims=True)
        dscores = (probs * (dprobs - delta)).astype(BF)
        dq = (dot(keys, dscores, TN) * scale).T
        d_ref[rows, cols] = dq.astype(BF)
        sum_ref[0:1, cols] += jnp.sum(dq, axis=0, keepdims=True)
        dk_acc[h] += dot(dscores, queries)
        dv_acc[h] += dot(probs.astype(BF), grads)

    @pl.when(step == pl.num_programs(0) - 1)
    def _():
        for h in range(heads):
            start = width + h * HDIM
            d_ref[:, start : start + HDIM] = (dk_acc[h] * scale).astype(BF)
            d_ref[:, width + start : width + start + HDIM] = dv_acc[h].astype(BF)
            sum_ref[1:2, h * HDIM : (h + 1) * HDIM] = jnp.sum(dv_acc[h], axis=0, keepdims=True)


def attend_back(x, grads, lse, tile):
    seq, width = x.shape[0], x.shape[1] // 3
    heads = width // HDIM
    whole = pl.BlockSpec((seq, 3 * width), lambda i: (0, 0))
    return pl.pallas_call(
        functools.partial(attend_back_kernel, heads, tile),
        grid=(seq // tile,),
        in_specs=[
            whole,
            pl.BlockSpec((tile, width), lambda i: (i, 0)),
            pl.BlockSpec((heads, tile), lambda i: (0, i)),
        ],
        out_specs=[whole, pl.BlockSpec((8, width), lambda i: (0, 0))],
        out_shape=[
            jax.ShapeDtypeStruct((seq, 3 * width), BF),
            jax.ShapeDtypeStruct((8, width), F32),
        ],
        scratch_shapes=[pltpu.VMEM((heads, seq, HDIM), F32), pltpu.VMEM((heads, seq, HDIM), F32)],
        cost_estimate=pl.CostEstimate(
            flops=10 * seq * seq * width,
            bytes_accessed=14 * seq * width,
            transcendentals=heads * seq * seq,
        ),
        name="attend_back",
    )(x, grads, lse)


def place_kernel(counts, cuts, table_ref, *refs):
    pieces, outs = refs[: len(counts)], refs[len(counts) :]
    start = 0
    for piece, count in zip(pieces, counts):

        def put(i, carry, piece=piece, start=start):
            for (low, high), out in zip(cuts, outs):
                cols = piece.shape[2]
                value = piece[i, low:high, :].astype(out.dtype)
                if out.shape[2] == cols:
                    out[table_ref[0, start + i]] = value
                else:
                    at = pl.multiple_of(table_ref[1, start + i] * cols, 128)
                    out[table_ref[0, start + i], :, pl.ds(at, cols)] = value
            return carry

        lax.fori_loop(0, count, put, 0)
        start += count


def place(pieces, row_of, outs, col_of=None, cuts=None):
    counts = [piece.shape[0] for piece in pieces]
    col_of = jnp.zeros_like(row_of) if col_of is None else col_of
    cuts = cuts or [(0, pieces[0].shape[1])]
    whole = pl.BlockSpec(memory_space=pltpu.VMEM)
    size = sum(2 * math.prod(x.shape) for x in pieces)
    return pl.pallas_call(
        functools.partial(place_kernel, counts, cuts),
        in_specs=[pl.BlockSpec(memory_space=pltpu.SMEM)] + [whole] * len(pieces),
        out_specs=[whole] * len(outs),
        out_shape=outs,
        cost_estimate=pl.CostEstimate(flops=0, bytes_accessed=3 * size, transcendentals=0),
        name="place",
    )(jnp.stack([row_of, col_of]).astype(jnp.int32), *pieces)


def heads_kernel(pair, width, place_ref, mine_ref, theirs_ref, out_ref):
    core, grp = place_ref[0], place_ref[1]
    rows = width // pair // 2
    for block in range(2 * pair):
        index = lax.rem(grp - block // 2 + pair * 2, pair)
        at = (0, lax.rem(index, pair // 2), block % 2)
        piece = jnp.where(core == index // (pair // 2), mine_ref[at], theirs_ref[at])
        for kind in range(3):
            start = kind * width + block * rows
            out_ref[0, :, start : start + rows] = piece[:, kind * rows : (kind + 1) * rows].astype(F32)


def place_heads(mine, theirs, core, grp, chip):
    chips, rounds, _, rows, cols = mine.shape
    pair = 2 * rounds
    width = cols // 3 * pair * 2
    piece = pl.BlockSpec((1, rounds, 2, rows, cols), lambda i, table: (i, 0, 0, 0, 0))
    return pl.pallas_call(
        functools.partial(heads_kernel, pair, width),
        grid_spec=pltpu.PrefetchScalarGridSpec(
            num_scalar_prefetch=1,
            grid=(chips,),
            in_specs=[piece, piece],
            out_specs=pl.BlockSpec((1, rows, 3 * width), lambda i, table: (table[2] ^ i, 0, 0)),
        ),
        out_shape=jax.ShapeDtypeStruct((chips, rows, 3 * width), F32),
        cost_estimate=pl.CostEstimate(
            flops=0, bytes_accessed=18 * chips * rows * width, transcendentals=0
        ),
        name="place_heads",
    )(jnp.stack([core, grp, chip]).astype(jnp.int32), mine, theirs)


def layer_norm(values):
    centre = values - jnp.mean(values, axis=-1, keepdims=True)
    inverse = lax.rsqrt(jnp.mean(centre * centre, axis=-1, keepdims=True) + EPS)
    return (centre * inverse, inverse)


def norm_back(normed, inverse, grad):
    return inverse * (
        grad
        - jnp.mean(grad, axis=-1, keepdims=True)
        - normed * jnp.mean(grad * normed, axis=-1, keepdims=True)
    )


def silu_float(values):
    return values * jax.nn.sigmoid(values)


def gelu_float(values):
    return jax.nn.gelu(values, approximate=True)


def shards(
    reps,
    grps,
    latents,
    condition,
    cotangent,
    ada_weight,
    ada_bias,
    qkv_weight,
    qv_bias,
    proj_weight,
    proj_bias,
    fc1_weight,
    fc1_bias,
    fc2_weight,
    fc2_bias,
):
    width = latents.shape[2]
    part = latents.shape[1]
    seq = part * grps
    rows = width // grps
    hidden_width = fc1_weight.shape[1]
    half = hidden_width // 2
    chips = reps // 2
    pair = grps // 2
    share = rows // chips
    fc2_rows = hidden_width // grps // chips
    rep, grp = lax.axis_index("rep"), lax.axis_index("grp")
    chip, core = rep // 2, rep % 2
    mesh_axes = ("rep", "grp")
    tile = min(256, seq)
    served = grp // pair
    block = grp % pair * 2 + core
    same_core = [[g * reps + r for g in range(grps) for r in range(c, reps, 2)] for c in range(2)]

    def shift(x, amount):
        return lax.ppermute(x, "grp", [(g, (g + amount) % grps) for g in range(grps)])

    def partner(x):
        return lax.ppermute(x, "rep", [(r, r ^ 1) for r in range(reps)])

    def hop(x, mask):
        return lax.ppermute(x, "rep", [(r, r ^ (2 * mask)) for r in range(reps)])

    def meeting(j):
        found = []
        for q in range(chips):
            for c in range(2):
                for g in range(grps):
                    here = (2 * q + c) * grps + g
                    there = (2 * q + g // pair) * grps + c * pair + (g + j) % pair
                    found.append((here, there))
        return found

    def pull(x, j):
        return lax.ppermute(x, mesh_axes, [(b, a) for a, b in meeting(j)])

    def push(x, j):
        return lax.ppermute(x, mesh_axes, meeting(j))

    rounds = (grp + jnp.arange(pair)) % pair
    order = chip ^ jnp.arange(chips)

    def turn(blocks, amount):
        twice = jnp.concatenate([blocks, blocks], axis=0)
        return lax.dynamic_slice_in_dim(twice, amount % grps, grps, 0)

    def exchange(blocks, sign):
        return [blocks[j] if j == 0 else shift(blocks[j], sign * j) for j in range(grps)]

    def own(array, index, count):
        return lax.dynamic_slice_in_dim(array, index * count, count, 0)

    def pick(array, index):
        return lax.dynamic_index_in_dim(array, index, 0, False)

    def add(terms):
        return sum(t.astype(F32) for t in terms).astype(BF)

    def spread(x):
        return [x] + [hop(x, m) for m in range(1, chips)]

    def scatter(blocks):
        mine = [lax.dynamic_index_in_dim(blocks, chip ^ m, 1, False) for m in range(chips)]
        return [mine[0]] + [hop(mine[m], m) for m in range(1, chips)]

    def to_owners(pieces):
        return [push(lax.dynamic_index_in_dim(pieces, (grp + j) % pair, 0, False), j) for j in range(pair)]

    def total(x):
        return jnp.sum(x, axis=0, keepdims=True)

    def after(x, *others):
        return lax.optimization_barrier((x, others))[0]

    cond_float = condition.astype(F32)
    cond_silu = silu_float(cond_float).astype(BF)
    cond_rows = lax.dynamic_slice_in_dim(cond_silu, grp * rows, rows, 1)
    biases = (ada_bias, qv_bias, proj_bias, fc1_bias, fc2_bias)
    small = jnp.concatenate([dot(cond_rows, ada_weight)] + [b.astype(F32)[None] for b in biases], axis=1)
    small = jnp.concatenate(exchange([small] * grps, -1))
    gathered = turn(small, grps - grp)
    mine = jnp.stack([push(latents[0], j) for j in range(pair)])
    tokens = jnp.concatenate([mine, partner(mine)]).reshape(seq, width)

    qkv_blocks = own(qkv_weight, chip, share).reshape(share, 3, pair, 2, rows)

    def heads_for(j):
        found = lax.dynamic_index_in_dim(qkv_blocks, (grp - j + grps) % pair, 2, False)
        return found.transpose(2, 0, 1, 3).reshape(2, share, 3 * rows)

    heads = jnp.stack([pull(heads_for(j), j) for j in range(pair)], axis=1)
    fc1_mine = lax.dynamic_slice(fc1_weight, (chip * share, core * half), (share, half))
    fc2_mine, proj_mine = own(fc2_weight, chip, fc2_rows), own(proj_weight, chip, share)
    fc1_mine, fc2_mine, proj_mine = after((fc1_mine, fc2_mine, proj_mine), mine, heads, small)
    proj_pulled = [pull(proj_mine, j) for j in range(pair)]
    fc2_pulled = [pull(fc2_mine, j) for j in range(pair)]
    heads = jnp.concatenate([pick(heads, core), partner(pick(heads, 1 - core))])
    both_pairs = jnp.concatenate([core * pair + rounds, (1 - core) * pair + rounds])
    (qkv_heads,) = place(
        spread(heads),
        (both_pairs[None, :] * chips + order[:, None]).reshape(-1),
        [jax.ShapeDtypeStruct((grps * chips, share, 3 * rows), BF)],
    )
    qkv_heads = qkv_heads.reshape(width, 3 * rows)

    parts = []
    start = 6 * width
    for b in biases:
        parts.append(gathered[:, start : start + b.shape[0]])
        start += b.shape[0]
    modulation = jnp.sum(gathered[:, : 6 * width], axis=0) + parts[0].reshape(-1)
    shift1, scale1, gate1, shift2, scale2, gate2 = [
        modulation[None, section * width : (section + 1) * width] for section in range(6)
    ]
    qv_own = lax.dynamic_index_in_dim(parts[1].reshape(2, grps, rows), block, 1, False)
    proj_bias_whole = parts[2].reshape(1, -1)
    fc1_bias_half = lax.dynamic_index_in_dim(parts[3].reshape(2, 1, half), core, 0, False)
    fc2_bias_whole = parts[4].reshape(1, -1)

    mod1 = modulation[None, : 2 * width]
    mod1 = jnp.where(served == core, mod1, partner(mod1))
    normed_all, _ = layer_norm(tokens.astype(F32))
    adapted_all = (normed_all * (1.0 + mod1[:, width:]) + mod1[:, :width]).astype(BF)
    qkv_bias = jnp.concatenate([qv_own[:1], jnp.zeros((1, rows), F32), qv_own[1:]], axis=1)
    projected = (dot(adapted_all, qkv_heads) + qkv_bias).astype(BF)
    proj_all = jnp.concatenate(spread(jnp.stack(after(proj_pulled, projected))))
    mixed, lse = attend(projected, tile)

    fc1_half = lax.all_gather(
        fc1_mine, ("grp", "rep"), axis=0, tiled=True, axis_index_groups=same_core
    )
    fc2_all = [x[None] for y in after(fc2_pulled, mixed) for x in spread(y)]
    here, there = mixed[: seq // 2], partner(mixed[seq // 2 :])
    mixed = jnp.stack([jnp.where(core == 0, here, there), jnp.where(core == 0, there, here)])
    mixed = mixed.reshape(2, pair, part, rows)
    mixed = jnp.stack([pull(mixed[:, j], j) for j in range(pair)])
    twice = jnp.concatenate([mixed, mixed])
    mixed = lax.dynamic_slice_in_dim(twice, (pair - grp % pair) % pair, pair, 0)
    attended = mixed.reshape(grps, part, rows).transpose(1, 0, 2).reshape(part, width)

    by_hop = (rounds[None, :] * chips + order[:, None]).reshape(-1)
    proj_all = after(proj_all, mixed)
    (proj_whole,) = place(
        [proj_all, partner(proj_all)],
        jnp.concatenate([core * pair * chips + by_hop, (1 - core) * pair * chips + by_hop]),
        [jax.ShapeDtypeStruct((grps * chips, share, width), BF)],
    )
    proj_whole = proj_whole.reshape(width, width)

    input_float = latents[0].astype(F32)
    grad_out = cotangent[0].astype(F32)
    attn_out = dot(attended, proj_whole) + proj_bias_whole
    middle = input_float + gate1 * attn_out
    normed2, inverse2 = layer_norm(middle)
    adapted2 = (normed2 * (1.0 + scale2) + shift2).astype(BF)
    grad_m = grad_out * gate2
    grad_m_b = grad_m.astype(BF)

    adapted_two = jnp.concatenate([adapted2, partner(adapted2)])
    grad_m_two = jnp.concatenate([grad_m_b, partner(grad_m_b)])
    hidden = dot(adapted_two, fc1_half) + fc1_bias_half
    activated = gelu_float(hidden).astype(BF)
    grad_fc2 = dot(activated, grad_m_two, TN).astype(BF)
    grad_fc2 = scatter(grad_fc2.reshape(pair, chips, fc2_rows, width))
    (fc2_half,) = place(
        after(fc2_all, activated),
        (rounds[:, None] * chips + order[None, :]).reshape(-1),
        [jax.ShapeDtypeStruct((pair * chips, fc2_rows, width), BF)],
    )
    fc2_half = fc2_half.reshape(half, width)
    mlp_two = dot(activated, fc2_half)
    mlp_out = mlp_two[:part] + partner(mlp_two[part:]) + fc2_bias_whole
    output = middle + gate2 * mlp_out
    grad_act = dot(grad_m_two, fc2_half, NT)
    grad_h = jax.vjp(gelu_float, hidden)[1](grad_act)[0]
    grad_h_b = grad_h.astype(BF)
    grad_fc1 = dot(adapted_two, grad_h_b, TN).astype(BF)
    grad_a2_two = dot(grad_h_b, fc1_half, NT)
    grad_a2 = grad_a2_two[:part] + partner(grad_a2_two[part:])

    grad_fc1 = scatter(grad_fc1.reshape(grps, chips, share, half))

    grad_mid = grad_out + norm_back(normed2, inverse2, grad_a2 * (1.0 + scale2))
    grad_att = grad_mid * gate1
    grad_att_b = grad_att.astype(BF)
    grad_o = dot(grad_att_b, proj_whole, NT).astype(BF)
    grad_o = grad_o.reshape(part, pair, 2, rows).transpose(1, 2, 0, 3)
    grad_o = jnp.stack([push(pick(grad_o, (grp + j) % pair), j) for j in range(pair)], axis=1)
    grad_o = jnp.concatenate([pick(grad_o, core), partner(pick(grad_o, 1 - core))]).reshape(seq, rows)

    grad_proj = dot(attended, grad_att_b, TN).astype(BF)
    grad_proj = add([own(grad_proj, core, width // 2), partner(own(grad_proj, 1 - core, width // 2))])
    grad_proj = scatter(grad_proj.reshape(pair, chips, share, width))

    grad_heads, qv_sums = attend_back(projected, grad_o, lse, tile)
    grad_a1 = dot(grad_heads, qkv_heads, NT)
    mod1_sums = jnp.concatenate([total(grad_a1), total(grad_a1 * normed_all)], axis=1)
    grad_a1 = grad_a1.astype(BF)
    grad_a1 = add([grad_a1[: seq // 2], partner(grad_a1[seq // 2 :])]).reshape(pair, part, width)
    grad_a1 = sum(pull(grad_a1[j], j).astype(F32) for j in range(pair))
    grad_fc2 = add(to_owners(add(after(grad_fc2, grad_heads))))
    grad_fc2 = add([own(grad_fc2, core, fc2_rows // 2), partner(own(grad_fc2, 1 - core, fc2_rows // 2))])
    fc2_all = jnp.stack(spread(grad_fc2))
    (grad_fc2_out,) = place(
        [fc2_all, partner(fc2_all)],
        jnp.concatenate([order * 2 + core, order * 2 + 1 - core]),
        [jax.ShapeDtypeStruct((2 * chips, fc2_rows // 2, width), F32)],
    )
    grad_fc1 = add(after(grad_fc1, mod1_sums))
    grad_fc1 = add(exchange(turn(grad_fc1, grp), 1))
    fc1_sums = jnp.stack(spread(grad_fc1))
    (grad_fc1_out,) = place(
        [fc1_sums, partner(fc1_sums)],
        jnp.concatenate([order, order]),
        [jax.ShapeDtypeStruct((chips, share, hidden_width), F32)],
        jnp.concatenate([core + 0 * order, 1 - core + 0 * order]),
    )

    grad_proj = add(to_owners(add(after(grad_proj, mod1_sums))))
    grad_proj = add([grad_proj, partner(grad_proj)])
    (grad_proj_out,) = place(
        [x[None] for x in spread(grad_proj)],
        order,
        [jax.ShapeDtypeStruct((chips, share, width), F32)],
    )

    normed1, inverse1 = layer_norm(input_float)
    grad_latents = grad_mid + norm_back(normed1, inverse1, grad_a1 * (1.0 + scale1))

    grad_qkv = dot(adapted_all, grad_heads, TN).astype(BF)
    here, there = own(grad_qkv, core, width // 2), partner(own(grad_qkv, 1 - core, width // 2))
    grad_qkv = jnp.stack([jnp.where(core == 0, here, there), jnp.where(core == 0, there, here)])
    grad_qkv = grad_qkv.reshape(2 * pair, chips, share, 3 * rows)
    grad_qkv = add(scatter(grad_qkv)).reshape(2, pair, share, 3 * rows).transpose(1, 0, 2, 3)
    grad_qkv = jnp.stack(to_owners(grad_qkv))
    grad_qkv = add([own(grad_qkv, core, pair // 2), partner(own(grad_qkv, 1 - core, pair // 2))])
    qkv_all = jnp.stack(spread(grad_qkv))
    grad_qkv_out = place_heads(qkv_all, partner(qkv_all), core, grp, chip)

    spread_h = lax.dynamic_update_slice_in_dim(
        jnp.zeros((1, hidden_width), F32), total(grad_h), core * half, 1
    )
    spread_qv = lax.dynamic_update_index_in_dim(
        jnp.zeros((2, grps, rows), F32), qv_sums[:2], block, 1
    )
    spread_mod1 = lax.dynamic_update_index_in_dim(jnp.zeros((2, 2 * width), F32), mod1_sums, served, 0)
    sums = jnp.concatenate(
        [
            total(grad_mid * attn_out),
            total(grad_a2),
            total(grad_a2 * normed2),
            total(grad_out * mlp_out),
            spread_qv.reshape(1, -1),
            total(grad_att),
            spread_h,
            total(grad_m),
            spread_mod1.reshape(1, -1),
        ],
        axis=1,
    )
    sums = sum(exchange([sums] * grps, 1))
    sums = jnp.concatenate([sums, cond_rows.astype(F32)], axis=1)
    other = partner(sums)
    ends = sums.shape[1] - 4 * width - rows, sums.shape[1] - rows
    mod1_sums = (sums + other)[:, ends[0] : ends[1]].reshape(2, 2 * width)

    def pair_up(own_rows, other_rows, upper):
        return jnp.concatenate(
            [jnp.where(upper, other_rows, own_rows), jnp.where(upper, own_rows, other_rows)]
        )

    sums = pair_up(sums, other, core == 1)
    sums = jnp.concatenate([mod1_sums, sums[:, : ends[0]], sums[:, ends[1] :]], axis=1)
    mod_own = lax.dynamic_slice_in_dim(sums, core, 1, 0)[:, : 6 * width]
    for bit in range(1, reps.bit_length() - 1):
        other = lax.ppermute(sums, "rep", [(r, r ^ (1 << bit)) for r in range(reps)])
        sums = pair_up(sums, other, (rep >> bit) % 2 == 1)
    grad_mod = sums[:, : 6 * width]
    cond_all = sums[:, sums.shape[1] - rows :]
    grad_ada = lax.dot_general(cond_all, grad_mod, TN, precision=lax.Precision.HIGHEST)
    grad_silu = lax.dot_general(mod_own, ada_weight.astype(F32), NT, precision=lax.Precision.HIGHEST)
    grad_silu = turn(jnp.concatenate(exchange([grad_silu] * grps, -1)), grps - grp).reshape(1, width)
    grad_condition = jax.vjp(silu_float, cond_float)[1](grad_silu)[0]

    bias_grads = []
    summed = total(sums)[0]
    start = 0
    for b in biases:
        count = b.shape[0]
        bias_grads.append(lax.dynamic_slice_in_dim(summed, start + grp * count, count))
        start += grps * count

    return (
        output[None],
        grad_latents[None],
        grad_condition,
        grad_ada,
        bias_grads[0],
        grad_qkv_out.reshape(rows, 3 * width),
        bias_grads[1],
        grad_proj_out.reshape(rows, width),
        bias_grads[2],
        grad_fc1_out.reshape(rows, hidden_width),
        bias_grads[3],
        grad_fc2_out.reshape(-1, width),
        bias_grads[4],
    )


def solution(mesh):
    tokens, vector, matrix = P("rep", "grp", None), P("grp"), P("grp", None)
    weights = (matrix, vector) * 5
    return jax.shard_map(
        functools.partial(shards, mesh.shape["rep"], mesh.shape["grp"]),
        mesh=mesh,
        in_specs=(tokens, P("rep", None), tokens) + weights,
        out_specs=(tokens, tokens, P("rep", None)) + weights,
        check_vma=False,
    )
```

```python
import functools
import math

import jax
import jax.numpy as jnp
from jax import lax
from jax.experimental import pallas as pl
from jax.experimental.pallas import tpu as pltpu
from jax.sharding import PartitionSpec as P


HDIM = 72
EPS = 1e-06
LOG2E = math.log2(math.e)
BF = jnp.bfloat16
F32 = jnp.float32
NT = (((1,), (1,)), ((), ()))
NN = (((1,), (0,)), ((), ()))
TN = (((0,), (0,)), ((), ()))


def dot(a, b, dims=NN):
    return lax.dot_general(a, b, dims, preferred_element_type=F32)


def parts_of(ref, rows, h):
    width = ref.shape[1] // 3
    return [ref[rows, k * width + h * HDIM : k * width + (h + 1) * HDIM] for k in range(3)]


def attend_kernel(heads, tile, x_ref, o_ref, lse_ref):
    factor = HDIM**-0.5 * LOG2E
    rows = pl.ds(pl.multiple_of(pl.program_id(0) * tile, tile), tile)
    for h in range(heads):
        queries = parts_of(x_ref, rows, h)[0]
        _, keys, values = parts_of(x_ref, slice(None), h)
        scores = dot(keys, queries, NT)
        top = jnp.max(scores, axis=0, keepdims=True)
        weights = jnp.exp2((scores - top) * factor)
        total = jnp.sum(weights, axis=0, keepdims=True)
        mixed = dot(values, weights.astype(BF), TN)
        o_ref[:, h * HDIM : (h + 1) * HDIM] = (mixed / total).T.astype(BF)
        lse_ref[h : h + 1, :] = top * factor + jnp.log2(total)


def attend(x, tile):
    seq, width = x.shape[0], x.shape[1] // 3
    heads = width // HDIM
    return pl.pallas_call(
        functools.partial(attend_kernel, heads, tile),
        grid=(seq // tile,),
        in_specs=[pl.BlockSpec((seq, 3 * width), lambda i: (0, 0))],
        out_specs=[
            pl.BlockSpec((tile, width), lambda i: (i, 0)),
            pl.BlockSpec((heads, tile), lambda i: (0, i)),
        ],
        out_shape=[
            jax.ShapeDtypeStruct((seq, width), BF),
            jax.ShapeDtypeStruct((heads, seq), F32),
        ],
        cost_estimate=pl.CostEstimate(
            flops=4 * seq * seq * width,
            bytes_accessed=8 * seq * width,
            transcendentals=heads * seq * seq,
        ),
        name="attend",
    )(x)


def attend_back_kernel(heads, tile, x_ref, g_ref, lse_ref, d_ref, sum_ref, dk_acc, dv_acc):
    step = pl.program_id(0)
    scale = HDIM**-0.5
    width = heads * HDIM
    rows = pl.ds(pl.multiple_of(step * tile, tile), tile)

    @pl.when(step == 0)
    def _():
        dk_acc[...] = jnp.zeros_like(dk_acc)
        dv_acc[...] = jnp.zeros_like(dv_acc)
        sum_ref[...] = jnp.zeros_like(sum_ref)

    for h in range(heads):
        cols = slice(h * HDIM, (h + 1) * HDIM)
        queries = parts_of(x_ref, rows, h)[0]
        _, keys, values = parts_of(x_ref, slice(None), h)
        grads = g_ref[:, cols]
        probs = jnp.exp2(dot(keys, queries, NT) * (scale * LOG2E) - lse_ref[h : h + 1, :])
        dprobs = dot(values, grads, NT)
        delta = jnp.sum(probs * dprobs, axis=0, keepdims=True)
        dscores = (probs * (dprobs - delta)).astype(BF)
        dq = (dot(keys, dscores, TN) * scale).T
        d_ref[rows, cols] = dq.astype(BF)
        sum_ref[0:1, cols] += jnp.sum(dq, axis=0, keepdims=True)
        dk_acc[h] += dot(dscores, queries)
        dv_acc[h] += dot(probs.astype(BF), grads)

    @pl.when(step == pl.num_programs(0) - 1)
    def _():
        for h in range(heads):
            start = width + h * HDIM
            d_ref[:, start : start + HDIM] = (dk_acc[h] * scale).astype(BF)
            d_ref[:, width + start : width + start + HDIM] = dv_acc[h].astype(BF)
            sum_ref[1:2, h * HDIM : (h + 1) * HDIM] = jnp.sum(dv_acc[h], axis=0, keepdims=True)


def attend_back(x, grads, lse, tile):
    seq, width = x.shape[0], x.shape[1] // 3
    heads = width // HDIM
    whole = pl.BlockSpec((seq, 3 * width), lambda i: (0, 0))
    return pl.pallas_call(
        functools.partial(attend_back_kernel, heads, tile),
        grid=(seq // tile,),
        in_specs=[
            whole,
            pl.BlockSpec((tile, width), lambda i: (i, 0)),
            pl.BlockSpec((heads, tile), lambda i: (0, i)),
        ],
        out_specs=[whole, pl.BlockSpec((8, width), lambda i: (0, 0))],
        out_shape=[
            jax.ShapeDtypeStruct((seq, 3 * width), BF),
            jax.ShapeDtypeStruct((8, width), F32),
        ],
        scratch_shapes=[pltpu.VMEM((heads, seq, HDIM), F32), pltpu.VMEM((heads, seq, HDIM), F32)],
        cost_estimate=pl.CostEstimate(
            flops=10 * seq * seq * width,
            bytes_accessed=14 * seq * width,
            transcendentals=heads * seq * seq,
        ),
        name="attend_back",
    )(x, grads, lse)


def place_kernel(counts, cuts, table_ref, *refs):
    pieces, outs = refs[: len(counts)], refs[len(counts) :]
    start = 0
    for piece, count in zip(pieces, counts):

        def put(i, carry, piece=piece, start=start):
            for k, ((low, high), out) in enumerate(zip(cuts, outs)):
                cols = piece.shape[2]
                value = piece[i, low:high, :].astype(out.dtype)
                row = table_ref[2 * k, start + i]
                if out.shape[2] == cols:
                    out[row] = value
                else:
                    out[row, :, pl.ds(pl.multiple_of(table_ref[2 * k + 1, start + i] * cols, 128), cols)] = value
            return carry

        lax.fori_loop(0, count, put, 0)
        start += count


def place(pieces, places, outs, cuts=None):
    counts = [piece.shape[0] for piece in pieces]
    places = [p if isinstance(p, tuple) else (p, jnp.zeros_like(p)) for p in places]
    cuts = cuts or [(0, pieces[0].shape[1])]
    whole = pl.BlockSpec(memory_space=pltpu.VMEM)
    size = sum(2 * math.prod(x.shape) for x in pieces)
    return pl.pallas_call(
        functools.partial(place_kernel, counts, cuts),
        in_specs=[pl.BlockSpec(memory_space=pltpu.SMEM)] + [whole] * len(pieces),
        out_specs=[whole] * len(outs),
        out_shape=outs,
        cost_estimate=pl.CostEstimate(flops=0, bytes_accessed=3 * size, transcendentals=0),
        name="place",
    )(jnp.stack([x for p in places for x in p]).astype(jnp.int32), *pieces)


def last_kernel(pair, width, place_ref, x_ref, proj_ref, qkv_ref):
    grp = place_ref[0]
    rows = width // pair // 2
    start = width // 2
    for core in range(2):
        proj_ref[0, :, core * start : (core + 1) * start] = x_ref[0, core, :, :start].astype(F32)
    for block in range(2 * pair):
        index = lax.rem(grp - block // 2 + pair * 2, pair)
        for at, sender in [(a, c) for a in range(pair) for c in range(2)]:
            first = start + (at % (pair // 2) * 2 + (block % 2 ^ sender)) * 3 * rows

            @pl.when((index == at) & (grp // pair == sender))
            def _():
                for kind in range(3):
                    qkv_ref[0, :, kind * width + block * rows : kind * width + (block + 1) * rows] = x_ref[
                        0, at // (pair // 2), :, first + kind * rows : first + (kind + 1) * rows
                    ].astype(F32)


def place_last(x, grp, pair, width):
    chips, _, share, cols = x.shape
    return pl.pallas_call(
        functools.partial(last_kernel, pair, width),
        grid_spec=pltpu.PrefetchScalarGridSpec(
            num_scalar_prefetch=1,
            grid=(chips,),
            in_specs=[pl.BlockSpec((1, 2, share, cols), lambda i, table: (i, 0, 0, 0))],
            out_specs=[
                pl.BlockSpec((1, share, width), lambda i, table: (i, 0, 0)),
                pl.BlockSpec((1, share, 3 * width), lambda i, table: (i, 0, 0)),
            ],
        ),
        out_shape=[
            jax.ShapeDtypeStruct((chips, share, width), F32),
            jax.ShapeDtypeStruct((chips, share, 3 * width), F32),
        ],
        cost_estimate=pl.CostEstimate(
            flops=0, bytes_accessed=24 * chips * share * width, transcendentals=0
        ),
        name="place_last",
    )(jnp.stack([grp]).astype(jnp.int32), x)


def take_columns_kernel(grps, place_ref, x_ref, out_ref):
    cols = out_ref.shape[1] // grps
    for rank in range(4):

        @pl.when(place_ref[0] == rank)
        def _():
            for block in range(grps):
                start = (4 * block + rank) * cols
                out_ref[:, block * cols : (block + 1) * cols] = x_ref[0, :, start : start + cols]


def take_columns(x, rank, line, grps):
    _, share, cols = x.shape
    return pl.pallas_call(
        functools.partial(take_columns_kernel, grps),
        grid_spec=pltpu.PrefetchScalarGridSpec(
            num_scalar_prefetch=1,
            grid=(1,),
            in_specs=[pl.BlockSpec((1, share, cols), lambda i, table: (table[1], 0, 0))],
            out_specs=pl.BlockSpec((share, cols // 4), lambda i, table: (0, 0)),
        ),
        out_shape=jax.ShapeDtypeStruct((share, cols // 4), BF),
        cost_estimate=pl.CostEstimate(flops=0, bytes_accessed=3 * share * cols, transcendentals=0),
        name="take_columns",
    )(jnp.stack([rank, line]).astype(jnp.int32), x)


def fc_kernel(fc1_rows, grps, x_ref, fc1_ref, fc2_ref):
    cols = x_ref.shape[3] // grps
    for rank in range(4):
        for block in range(grps):
            start = (4 * block + rank) * cols
            fc1_ref[0, :, start : start + cols] = x_ref[
                0, rank, :fc1_rows, block * cols : (block + 1) * cols
            ].astype(F32)
        fc2_ref[rank, 0] = x_ref[0, rank, fc1_rows:, :].astype(F32)


def place_fc(x, fc1_rows, grps):
    lines, _, both, cols = x.shape
    fc2_rows = both - fc1_rows
    return pl.pallas_call(
        functools.partial(fc_kernel, fc1_rows, grps),
        grid=(lines,),
        in_specs=[pl.BlockSpec((1, 4, both, cols), lambda i: (i, 0, 0, 0))],
        out_specs=[
            pl.BlockSpec((1, fc1_rows, 4 * cols), lambda i: (i, 0, 0)),
            pl.BlockSpec((4, 1, fc2_rows, cols), lambda i: (0, i, 0, 0)),
        ],
        out_shape=[
            jax.ShapeDtypeStruct((lines, fc1_rows, 4 * cols), F32),
            jax.ShapeDtypeStruct((4, lines, fc2_rows, cols), F32),
        ],
        cost_estimate=pl.CostEstimate(
            flops=0, bytes_accessed=24 * lines * both * cols, transcendentals=0
        ),
        name="place_fc",
    )(x)


def take_heads_kernel(pair, place_ref, x_ref, out_ref):
    grp = place_ref[1]
    width = x_ref.shape[2] // 3
    rows = width // pair // 2
    for unit in range(pair):
        index = lax.rem(grp - unit + pair * 2, pair)
        for core in range(2):
            for kind in range(3):
                start = kind * width + (2 * unit + core) * rows
                out_ref[index, core, :, kind * rows : (kind + 1) * rows] = x_ref[0, :, start : start + rows]


def heads_for(x, core, grp, chip):
    _, share, cols = x.shape
    grps = lax.axis_size("grp")
    rows = cols // 3 // grps
    return pl.pallas_call(
        functools.partial(take_heads_kernel, grps // 2),
        grid_spec=pltpu.PrefetchScalarGridSpec(
            num_scalar_prefetch=1,
            grid=(1,),
            in_specs=[pl.BlockSpec((1, share, cols), lambda i, table: (table[2], 0, 0))],
            out_specs=pl.BlockSpec((grps // 2, 2, share, 3 * rows), lambda i, table: (0, 0, 0, 0)),
        ),
        out_shape=jax.ShapeDtypeStruct((grps // 2, 2, share, 3 * rows), BF),
        cost_estimate=pl.CostEstimate(flops=0, bytes_accessed=4 * share * cols, transcendentals=0),
        name="take_heads",
    )(jnp.stack([core, grp, chip]).astype(jnp.int32), x)


def layer_norm(values):
    centre = values - jnp.mean(values, axis=-1, keepdims=True)
    inverse = lax.rsqrt(jnp.mean(centre * centre, axis=-1, keepdims=True) + EPS)
    return (centre * inverse, inverse)


def norm_back(normed, inverse, grad):
    return inverse * (
        grad
        - jnp.mean(grad, axis=-1, keepdims=True)
        - normed * jnp.mean(grad * normed, axis=-1, keepdims=True)
    )


def silu_float(values):
    return values * jax.nn.sigmoid(values)


def gelu_float(values):
    return jax.nn.gelu(values, approximate=True)


def block_step(
    reps,
    grps,
    latents,
    condition,
    cotangent,
    ada_weight,
    ada_bias,
    qkv_weight,
    qv_bias,
    proj_weight,
    proj_bias,
    fc1_weight,
    fc1_bias,
    fc2_weight,
    fc2_bias,
):
    width = latents.shape[2]
    part = latents.shape[1]
    seq = part * grps
    rows = width // grps
    hidden_width = fc1_weight.shape[1]
    chips = reps // 2
    pair = grps // 2
    share = rows // chips
    rep, grp = lax.axis_index("rep"), lax.axis_index("grp")
    chip, core = rep // 2, rep % 2
    quarter = hidden_width // 4
    mesh_axes = ("rep", "grp")
    tile = min(256, seq)
    served = grp // pair
    block = grp % pair * 2 + core
    lines = reps // 4
    line, rank = rep // 4, rep % 4
    fc1_rows, fc2_rows = rows // lines, quarter // grps // lines
    same_rank = [[g * reps + r for g in range(grps) for r in range(f, reps, 4)] for f in range(4)]

    def shift(x, amount):
        return lax.ppermute(x, "grp", [(g, (g + amount) % grps) for g in range(grps)])

    def partner(x):
        return lax.ppermute(x, "rep", [(r, r ^ 1) for r in range(reps)])

    def hop(x, mask):
        return lax.ppermute(x, "rep", [(r, r ^ (2 * mask)) for r in range(reps)])

    def meeting(j):
        found = []
        for q in range(chips):
            for c in range(2):
                for g in range(grps):
                    here = (2 * q + c) * grps + g
                    there = (2 * q + g // pair) * grps + c * pair + (g + j) % pair
                    found.append((here, there))
        return found

    def pull(x, j):
        return lax.ppermute(x, mesh_axes, [(b, a) for a, b in meeting(j)])

    def push(x, j):
        return lax.ppermute(x, mesh_axes, meeting(j))

    rounds = (grp + jnp.arange(pair)) % pair
    order = chip ^ jnp.arange(chips)

    def turn(blocks, amount):
        twice = jnp.concatenate([blocks, blocks], axis=0)
        return lax.dynamic_slice_in_dim(twice, amount % grps, grps, 0)

    def exchange(x, sign):
        return [x if j == 0 else shift(x, sign * j) for j in range(grps)]

    def own(array, index, count):
        return lax.dynamic_slice_in_dim(array, index * count, count, 0)

    def pick(array, index):
        return lax.dynamic_index_in_dim(array, index, 0, False)

    def add(terms):
        return sum(t.astype(F32) for t in terms).astype(BF)

    def spread(x):
        return [x] + [hop(x, m) for m in range(1, chips)]

    def scatter(blocks):
        mine = [lax.dynamic_index_in_dim(blocks, chip ^ m, 1, False) for m in range(chips)]
        return [mine[0]] + [hop(mine[m], m) for m in range(1, chips)]

    def to_owners(pieces):
        return [push(pick(pieces, (grp + j) % pair), j) for j in range(pair)]

    def split3(x):
        high = lax.reduce_precision(x, 8, 7)
        middle = lax.reduce_precision(x - high, 8, 7)
        return jnp.concatenate([high, middle, x - high - middle]).astype(BF)

    def total(x):
        return jnp.sum(x, axis=0, keepdims=True)

    def four(x):
        far = hop(x, 1)
        return jnp.concatenate([x, partner(x), far, partner(far)])

    def four_sum(x):
        x = x.astype(BF).reshape(4, part, width)
        far = add([x[2], partner(x[3])])
        near = x[0].astype(F32) + partner(x[1]).astype(F32)
        return near + hop(far, 1).astype(F32), far

    def line_sum(blocks):
        mine = list(lax.optimization_barrier([lax.dynamic_index_in_dim(blocks, line ^ m, 1, False) for m in range(lines)]))
        return [mine[0]] + [hop(mine[m], 2 * m) for m in range(1, lines)]

    def grp_sum(blocks):
        turned = turn(blocks, grp)
        return [turned[j] if j == 0 else shift(turned[j], j) for j in range(grps)]

    def after(x, *others):
        return lax.optimization_barrier((x, others))[0]

    cond_float = condition.astype(F32)
    cond_silu = silu_float(cond_float).astype(BF)
    cond_rows = lax.dynamic_slice_in_dim(cond_silu, grp * rows, rows, 1)
    biases = (ada_bias, qv_bias, proj_bias, fc1_bias, fc2_bias)
    small = jnp.concatenate(
        [dot(cond_rows, ada_weight), jnp.concatenate(biases).astype(F32)[None]], axis=1
    )
    heads = heads_for(qkv_weight.reshape(chips, share, 3 * width), core, grp, chip)
    fc1_mine = take_columns(fc1_weight.reshape(lines, fc1_rows, hidden_width), rank, line, grps)
    fc2_mine = own(fc2_weight, rank * lines + line, fc2_rows)
    fc_mine = jnp.concatenate([fc1_mine, fc2_mine])
    heads, small = after((heads, small), fc_mine)
    small = after(small, heads)
    small = jnp.concatenate(exchange(small, -1))
    gathered = turn(small, grps - grp)
    heads = [pull(heads[j], j) for j in range(pair)]
    mine = jnp.stack([push(latents[0], j) for j in range(pair)])
    tokens = jnp.concatenate([mine, partner(mine)]).reshape(seq, width)

    fc_quarter = lax.all_gather(fc_mine, ("grp", "rep"), axis=0, axis_index_groups=same_rank)
    fc1_quarter = fc_quarter[:, :fc1_rows].reshape(width, quarter)
    fc2_quarter = fc_quarter[:, fc1_rows:].reshape(quarter, width)

    proj_mine = after(own(proj_weight, chip, share), mine, heads, small)
    proj_pulled = [pull(proj_mine, j) for j in range(pair)]
    heads = [jnp.stack([pick(x, core) for x in heads]), jnp.stack([pick(x, 1 - core) for x in heads])]
    heads = jnp.concatenate([heads[0], partner(heads[1])])
    both_pairs = jnp.concatenate([core * pair + rounds, (1 - core) * pair + rounds])
    (qkv_heads,) = place(
        spread(heads),
        [(both_pairs[None, :] * chips + order[:, None]).reshape(-1)],
        [jax.ShapeDtypeStruct((grps * chips, share, 3 * rows), BF)],
    )
    qkv_heads = qkv_heads.reshape(width, 3 * rows)

    parts = []
    start = 6 * width
    for b in biases:
        parts.append(gathered[:, start : start + b.shape[0]])
        start += b.shape[0]
    modulation = jnp.sum(gathered[:, : 6 * width], axis=0) + parts[0].reshape(-1)
    _, scale1, gate1, shift2, scale2, gate2 = [
        modulation[None, section * width : (section + 1) * width] for section in range(6)
    ]
    qv_own = lax.dynamic_index_in_dim(parts[1].reshape(2, grps, rows), block, 1, False)
    proj_bias_whole = parts[2].reshape(1, -1)
    fc1_bias_part = lax.dynamic_index_in_dim(parts[3].reshape(grps, 4, -1), rank, 1, False).reshape(1, -1)
    fc2_bias_whole = parts[4].reshape(1, -1)

    mod1 = modulation[None, : 2 * width]
    mod1 = jnp.where(served == core, mod1, partner(mod1))
    normed_all, _ = layer_norm(tokens.astype(F32))
    adapted_all = (normed_all * (1.0 + mod1[:, width:]) + mod1[:, :width]).astype(BF)
    qkv_bias = jnp.concatenate([qv_own[:1], jnp.zeros((1, rows), F32), qv_own[1:]], axis=1)
    projected = (dot(adapted_all, qkv_heads) + qkv_bias).astype(BF)
    proj_all = spread(jnp.stack(after(proj_pulled, projected)))
    mixed, lse = attend(projected, tile)

    here, there = mixed[: seq // 2], partner(mixed[seq // 2 :])
    mixed = jnp.stack([jnp.where(core == 0, here, there), jnp.where(core == 0, there, here)])
    mixed = mixed.reshape(2, pair, part, rows)
    mixed = jnp.stack([pull(mixed[:, j], j) for j in range(pair)])
    twice = jnp.concatenate([mixed, mixed])
    mixed = lax.dynamic_slice_in_dim(twice, (pair - grp % pair) % pair, pair, 0)
    attended = mixed.reshape(grps, part, rows).transpose(1, 0, 2).reshape(part, width)

    by_hop = (rounds[None, :] * chips + order[:, None]).reshape(-1)
    proj_all = after(proj_all, mixed)
    (proj_whole,) = place(
        proj_all + [partner(x) for x in proj_all],
        [jnp.concatenate([core * pair * chips + by_hop, (1 - core) * pair * chips + by_hop])],
        [jax.ShapeDtypeStruct((grps * chips, share, width), BF)],
    )
    proj_whole = proj_whole.reshape(width, width)

    input_float = latents[0].astype(F32)
    grad_out = cotangent[0].astype(F32)
    attn_out = dot(attended, proj_whole) + proj_bias_whole
    middle = input_float + gate1 * attn_out
    normed2, inverse2 = layer_norm(middle)
    adapted2 = (normed2 * (1.0 + scale2) + shift2).astype(BF)
    grad_m = grad_out * gate2
    grad_m_b = grad_m.astype(BF)

    grad_m_four = four(grad_m_b)
    adapted_four = four(adapted2)
    grad_act = dot(grad_m_four, fc2_quarter, NT)
    hidden = dot(adapted_four, fc1_quarter) + fc1_bias_part
    activated = gelu_float(hidden).astype(BF)
    grad_h = jax.vjp(gelu_float, hidden)[1](grad_act)[0]
    grad_h_b = grad_h.astype(BF)
    grad_a2, far = four_sum(dot(grad_h_b, fc1_quarter, NT))
    adapted_four, activated, grad_m_four = after((adapted_four, activated, grad_m_four), far)
    grad_fc2 = dot(activated, grad_m_four, TN).astype(BF).reshape(grps, lines, fc2_rows, width)
    grad_fc2 = line_sum(grad_fc2)
    adapted_four = after(adapted_four, grad_fc2[0])
    grad_fc1 = dot(adapted_four, grad_h_b, TN).astype(BF)
    grad_fc1 = grad_fc1.reshape(grps, lines, fc1_rows, quarter)
    grad_fc1 = line_sum(grad_fc1)

    grad_mid = grad_out + norm_back(normed2, inverse2, grad_a2 * (1.0 + scale2))
    grad_att = grad_mid * gate1
    grad_att_b = grad_att.astype(BF)
    grad_o = dot(grad_att_b, proj_whole, NT).astype(BF)
    grad_o = grad_o.reshape(part, pair, 2, rows).transpose(1, 2, 0, 3)
    grad_o = [pick(grad_o, (grp + j) % pair) for j in range(pair)]
    mlp_out = dot(after(activated, grad_o), fc2_quarter)
    mlp_out, _ = four_sum(mlp_out)
    mlp_out = mlp_out + fc2_bias_whole
    output = middle + gate2 * mlp_out
    grad_o = jnp.stack([push(x, j) for j, x in enumerate(grad_o)], axis=1)
    grad_o = jnp.concatenate([pick(grad_o, core), partner(pick(grad_o, 1 - core))]).reshape(seq, rows)

    grad_proj = dot(attended, grad_att_b, TN).astype(BF)
    grad_proj = add([own(grad_proj, core, width // 2), partner(own(grad_proj, 1 - core, width // 2))])
    grad_proj = scatter(grad_proj.reshape(pair, chips, share, width))

    grad_fc2 = grp_sum(add(after(grad_fc2, grad_o)))
    grad_fc1 = grp_sum(add(after(grad_fc1, grad_o)))
    grad_heads, qv_sums = attend_back(projected, grad_o, lse, tile)
    grad_qkv = dot(adapted_all, grad_heads, TN).astype(BF)
    here, there = own(grad_qkv, core, width // 2), partner(own(grad_qkv, 1 - core, width // 2))
    grad_heads = after(grad_heads, here)
    grad_a1 = dot(grad_heads, qkv_heads, NT)
    mod1_sums = jnp.concatenate([total(grad_a1), total(grad_a1 * normed_all)], axis=1)
    grad_a1 = grad_a1.astype(BF)
    grad_a1 = add([grad_a1[: seq // 2], partner(grad_a1[seq // 2 :])]).reshape(pair, part, width)
    grad_a1 = sum(pull(grad_a1[j], j).astype(F32) for j in range(pair))
    fc_sums = jnp.concatenate([add(after(grad_fc1, mod1_sums)), add(after(grad_fc2, mod1_sums))])
    fc_sums = lax.all_gather(fc_sums, "rep", axis=0)
    grad_fc1_out, grad_fc2_out = place_fc(fc_sums.reshape(lines, 4, -1, width), fc1_rows, grps)

    grad_proj = add(to_owners(add(after(grad_proj, grad_heads))))
    grad_proj = add([grad_proj, partner(grad_proj)])

    normed1, inverse1 = layer_norm(input_float)
    grad_latents = grad_mid + norm_back(normed1, inverse1, grad_a1 * (1.0 + scale1))

    here, there = [x.reshape(pair, chips, share, 3 * rows) for x in (here, there)]
    grad_qkv = [
        jnp.stack([lax.dynamic_index_in_dim(x, chip ^ m, 1, False) for x in (here, there)], axis=1)
        for m in range(chips)
    ]
    grad_qkv = add([grad_qkv[0]] + [hop(grad_qkv[m], m) for m in range(1, chips)])
    grad_qkv = jnp.stack(to_owners(grad_qkv))
    grad_qkv = add([own(grad_qkv, core, pair // 2), partner(own(grad_qkv, 1 - core, pair // 2))])
    last = jnp.concatenate(
        [
            lax.dynamic_slice_in_dim(grad_proj, core * (width // 2), width // 2, 1),
            grad_qkv.transpose(2, 0, 1, 3).reshape(share, -1),
        ],
        axis=1,
    )
    last = lax.all_gather(last, "rep", axis=0)
    grad_proj_out, grad_qkv_out = place_last(last.reshape(chips, 2, share, -1), grp, pair, width)

    spread_h = lax.dynamic_update_index_in_dim(
        jnp.zeros((grps, 4, quarter // grps), F32), total(grad_h).reshape(grps, -1), rank, 1
    ).reshape(1, -1)
    spread_qv = lax.dynamic_update_index_in_dim(
        jnp.zeros((2, grps, rows), F32), qv_sums[:2], block, 1
    )
    spread_mod1 = lax.dynamic_update_index_in_dim(jnp.zeros((2, 2 * width), F32), mod1_sums, served, 0)
    sums = jnp.concatenate(
        [
            total(grad_mid * attn_out),
            total(grad_a2),
            total(grad_a2 * normed2),
            total(grad_out * mlp_out),
            spread_qv.reshape(1, -1),
            total(grad_att),
            spread_h,
            total(grad_m),
            spread_mod1.reshape(1, -1),
        ],
        axis=1,
    )
    sums = sum(exchange(sums, 1))
    sums = jnp.concatenate([sums, cond_rows.astype(F32)], axis=1)
    other = partner(sums)
    ends = sums.shape[1] - 4 * width - rows, sums.shape[1] - rows
    mod1_sums = (sums + other)[:, ends[0] : ends[1]].reshape(2, 2 * width)

    def pair_up(own_rows, other_rows, upper):
        return jnp.concatenate(
            [jnp.where(upper, other_rows, own_rows), jnp.where(upper, own_rows, other_rows)]
        )

    sums = pair_up(sums, other, core == 1)
    sums = jnp.concatenate([mod1_sums, sums[:, : ends[0]], sums[:, ends[1] :]], axis=1)
    mod_own = lax.dynamic_slice_in_dim(sums, core, 1, 0)[:, : 6 * width]
    for bit in range(1, reps.bit_length() - 1):
        other = hop(sums, 1 << (bit - 1))
        sums = pair_up(sums, other, (rep >> bit) % 2 == 1)
    grad_mod = sums[:, : 6 * width]
    cond_all = sums[:, sums.shape[1] - rows :]
    grad_ada = dot(jnp.concatenate([cond_all.astype(BF)] * 3), split3(grad_mod), TN)
    grad_silu = total(dot(split3(mod_own), ada_weight, NT))
    grad_silu = after(jnp.concatenate(exchange(grad_silu, -1)), grad_qkv)
    grad_silu = turn(grad_silu, grps - grp).reshape(1, width)
    grad_condition = jax.vjp(silu_float, cond_float)[1](grad_silu)[0]

    bias_grads = []
    summed = total(sums)[0]
    start = 0
    for b in biases:
        count = b.shape[0]
        bias_grads.append(lax.dynamic_slice_in_dim(summed, start + grp * count, count))
        start += grps * count

    return (
        output[None],
        grad_latents[None],
        grad_condition,
        grad_ada,
        bias_grads[0],
        grad_qkv_out.reshape(rows, 3 * width),
        bias_grads[1],
        grad_proj_out.reshape(rows, width),
        bias_grads[2],
        grad_fc1_out.reshape(rows, hidden_width),
        bias_grads[3],
        grad_fc2_out.reshape(-1, width),
        bias_grads[4],
    )


def solution(mesh):
    tokens, vector, matrix = P("rep", "grp", None), P("grp"), P("grp", None)
    weights = (matrix, vector) * 5
    return jax.shard_map(
        functools.partial(block_step, mesh.shape["rep"], mesh.shape["grp"]),
        mesh=mesh,
        in_specs=(tokens, P("rep", None), tokens) + weights,
        out_specs=(tokens, tokens, P("rep", None)) + weights,
        check_vma=False,
    )
```

```python
import functools
import math

import jax
import jax.numpy as jnp
from jax import lax
from jax.experimental import pallas as pl
from jax.experimental.pallas import tpu as pltpu
from jax.experimental.layout import Layout, with_layout_constraint
from jax.sharding import PartitionSpec as P


HDIM = 72
EPS = 1e-06
LOG2E = math.log2(math.e)
BF = jnp.bfloat16
F32 = jnp.float32
NT = (((1,), (1,)), ((), ()))
NN = (((1,), (0,)), ((), ()))
TN = (((0,), (0,)), ((), ()))


def dot(a, b, dims=NN):
    return lax.dot_general(a, b, dims, preferred_element_type=F32)


def parts_of(ref, rows, h):
    width = ref.shape[1] // 3
    return [ref[rows, k * width + h * HDIM : k * width + (h + 1) * HDIM] for k in range(3)]


def attend_kernel(heads, tile, x_ref, o_ref, lse_ref):
    factor = HDIM**-0.5 * LOG2E
    rows = pl.ds(pl.multiple_of(pl.program_id(0) * tile, tile), tile)
    for h in range(heads):
        queries = parts_of(x_ref, rows, h)[0]
        _, keys, values = parts_of(x_ref, slice(None), h)
        scores = dot(keys, queries, NT)
        top = jnp.max(scores, axis=0, keepdims=True)
        weights = jnp.exp2((scores - top) * factor)
        total = jnp.sum(weights, axis=0, keepdims=True)
        mixed = dot(values, weights.astype(BF), TN)
        o_ref[:, h * HDIM : (h + 1) * HDIM] = (mixed / total).T.astype(BF)
        lse_ref[h : h + 1, :] = top * factor + jnp.log2(total)


def attend(x, tile):
    seq, width = x.shape[0], x.shape[1] // 3
    heads = width // HDIM
    return pl.pallas_call(
        functools.partial(attend_kernel, heads, tile),
        grid=(seq // tile,),
        in_specs=[pl.BlockSpec((seq, 3 * width), lambda i: (0, 0))],
        out_specs=[
            pl.BlockSpec((tile, width), lambda i: (i, 0)),
            pl.BlockSpec((heads, tile), lambda i: (0, i)),
        ],
        out_shape=[
            jax.ShapeDtypeStruct((seq, width), BF),
            jax.ShapeDtypeStruct((heads, seq), F32),
        ],
        cost_estimate=pl.CostEstimate(
            flops=4 * seq * seq * width,
            bytes_accessed=8 * seq * width,
            transcendentals=heads * seq * seq,
        ),
        name="attend",
    )(x)


def attend_back_kernel(heads, tile, x_ref, g_ref, lse_ref, d_ref, sum_ref, dk_acc, dv_acc):
    step = pl.program_id(0)
    scale = HDIM**-0.5
    width = heads * HDIM
    rows = pl.ds(pl.multiple_of(step * tile, tile), tile)

    @pl.when(step == 0)
    def _():
        dk_acc[...] = jnp.zeros_like(dk_acc)
        dv_acc[...] = jnp.zeros_like(dv_acc)
        sum_ref[...] = jnp.zeros_like(sum_ref)

    for h in range(heads):
        cols = slice(h * HDIM, (h + 1) * HDIM)
        queries = parts_of(x_ref, rows, h)[0]
        _, keys, values = parts_of(x_ref, slice(None), h)
        grads = g_ref[:, cols]
        probs = jnp.exp2(dot(keys, queries, NT) * (scale * LOG2E) - lse_ref[h : h + 1, :])
        dprobs = dot(values, grads, NT)
        delta = jnp.sum(probs * dprobs, axis=0, keepdims=True)
        dscores = (probs * (dprobs - delta)).astype(BF)
        dq = (dot(keys, dscores, TN) * scale).T
        d_ref[rows, cols] = dq.astype(BF)
        sum_ref[0:1, cols] += jnp.sum(dq, axis=0, keepdims=True)
        dk_acc[h] += dot(dscores, queries)
        dv_acc[h] += dot(probs.astype(BF), grads)

    @pl.when(step == pl.num_programs(0) - 1)
    def _():
        for h in range(heads):
            start = width + h * HDIM
            d_ref[:, start : start + HDIM] = (dk_acc[h] * scale).astype(BF)
            d_ref[:, width + start : width + start + HDIM] = dv_acc[h].astype(BF)
            sum_ref[1:2, h * HDIM : (h + 1) * HDIM] = jnp.sum(dv_acc[h], axis=0, keepdims=True)


def attend_back(x, grads, lse, tile):
    seq, width = x.shape[0], x.shape[1] // 3
    heads = width // HDIM
    whole = pl.BlockSpec((seq, 3 * width), lambda i: (0, 0))
    return pl.pallas_call(
        functools.partial(attend_back_kernel, heads, tile),
        grid=(seq // tile,),
        in_specs=[
            whole,
            pl.BlockSpec((tile, width), lambda i: (i, 0)),
            pl.BlockSpec((heads, tile), lambda i: (0, i)),
        ],
        out_specs=[whole, pl.BlockSpec((8, width), lambda i: (0, 0))],
        out_shape=[
            jax.ShapeDtypeStruct((seq, 3 * width), BF),
            jax.ShapeDtypeStruct((8, width), F32),
        ],
        scratch_shapes=[pltpu.VMEM((heads, seq, HDIM), F32), pltpu.VMEM((heads, seq, HDIM), F32)],
        cost_estimate=pl.CostEstimate(
            flops=10 * seq * seq * width,
            bytes_accessed=14 * seq * width,
            transcendentals=heads * seq * seq,
        ),
        name="attend_back",
    )(x, grads, lse)


def place_kernel(counts, cuts, table_ref, *refs):
    pieces, outs = refs[: len(counts)], refs[len(counts) :]
    start = 0
    for piece, count in zip(pieces, counts):

        def put(i, carry, piece=piece, start=start):
            for k, ((low, high), out) in enumerate(zip(cuts, outs)):
                cols = piece.shape[2]
                value = piece[i, low:high, :].astype(out.dtype)
                row = table_ref[2 * k, start + i]
                if out.shape[2] == cols:
                    out[row] = value
                else:
                    out[row, :, pl.ds(pl.multiple_of(table_ref[2 * k + 1, start + i] * cols, 128), cols)] = value
            return carry

        lax.fori_loop(0, count, put, 0)
        start += count


def place(pieces, places, outs, cuts=None):
    counts = [piece.shape[0] for piece in pieces]
    places = [p if isinstance(p, tuple) else (p, jnp.zeros_like(p)) for p in places]
    cuts = cuts or [(0, pieces[0].shape[1])]
    whole = pl.BlockSpec(memory_space=pltpu.VMEM)
    size = sum(2 * math.prod(x.shape) for x in pieces)
    return pl.pallas_call(
        functools.partial(place_kernel, counts, cuts),
        in_specs=[pl.BlockSpec(memory_space=pltpu.SMEM)] + [whole] * len(pieces),
        out_specs=[whole] * len(outs),
        out_shape=outs,
        cost_estimate=pl.CostEstimate(flops=0, bytes_accessed=3 * size, transcendentals=0),
        name="place",
    )(jnp.stack([x for p in places for x in p]).astype(jnp.int32), *pieces)


def last_kernel(pair, width, place_ref, x_ref, proj_ref, qkv_ref):
    grp = place_ref[0]
    rows = width // pair // 2
    start = width // 2
    for core in range(2):
        proj_ref[0, :, core * start : (core + 1) * start] = x_ref[0, core, :, :start].astype(F32)
    for block in range(2 * pair):
        index = lax.rem(grp - block // 2 + pair * 2, pair)
        for at, sender in [(a, c) for a in range(pair) for c in range(2)]:
            first = start + (at % (pair // 2) * 2 + (block % 2 ^ sender)) * 3 * rows

            @pl.when((index == at) & (grp // pair == sender))
            def _():
                for kind in range(3):
                    qkv_ref[0, :, kind * width + block * rows : kind * width + (block + 1) * rows] = x_ref[
                        0, at // (pair // 2), :, first + kind * rows : first + (kind + 1) * rows
                    ].astype(F32)


def place_last(x, grp, pair, width):
    chips, _, share, cols = x.shape
    return pl.pallas_call(
        functools.partial(last_kernel, pair, width),
        grid_spec=pltpu.PrefetchScalarGridSpec(
            num_scalar_prefetch=1,
            grid=(chips,),
            in_specs=[pl.BlockSpec((1, 2, share, cols), lambda i, table: (i, 0, 0, 0))],
            out_specs=[
                pl.BlockSpec((1, share, width), lambda i, table: (i, 0, 0)),
                pl.BlockSpec((1, share, 3 * width), lambda i, table: (i, 0, 0)),
            ],
        ),
        out_shape=[
            jax.ShapeDtypeStruct((chips, share, width), F32),
            jax.ShapeDtypeStruct((chips, share, 3 * width), F32),
        ],
        cost_estimate=pl.CostEstimate(
            flops=0, bytes_accessed=24 * chips * share * width, transcendentals=0
        ),
        name="place_last",
    )(jnp.stack([grp]).astype(jnp.int32), x)


def take_columns_kernel(grps, place_ref, x_ref, out_ref):
    cols = out_ref.shape[1] // grps
    for rank in range(4):

        @pl.when(place_ref[0] == rank)
        def _():
            for block in range(grps):
                start = (4 * block + rank) * cols
                out_ref[:, block * cols : (block + 1) * cols] = x_ref[0, :, start : start + cols]


def take_columns(x, rank, line, grps):
    _, share, cols = x.shape
    return pl.pallas_call(
        functools.partial(take_columns_kernel, grps),
        grid_spec=pltpu.PrefetchScalarGridSpec(
            num_scalar_prefetch=1,
            grid=(1,),
            in_specs=[pl.BlockSpec((1, share, cols), lambda i, table: (table[1], 0, 0))],
            out_specs=pl.BlockSpec((share, cols // 4), lambda i, table: (0, 0)),
        ),
        out_shape=jax.ShapeDtypeStruct((share, cols // 4), BF),
        cost_estimate=pl.CostEstimate(flops=0, bytes_accessed=3 * share * cols, transcendentals=0),
        name="take_columns",
    )(jnp.stack([rank, line]).astype(jnp.int32), x)


def fc_kernel(fc1_rows, grps, x_ref, fc1_ref, fc2_ref):
    cols = x_ref.shape[3] // grps
    for rank in range(4):
        for block in range(grps):
            start = (4 * block + rank) * cols
            fc1_ref[0, :, start : start + cols] = x_ref[
                0, rank, :fc1_rows, block * cols : (block + 1) * cols
            ].astype(F32)
        fc2_ref[rank, 0] = x_ref[0, rank, fc1_rows:, :].astype(F32)


def place_fc(x, fc1_rows, grps):
    lines, _, both, cols = x.shape
    fc2_rows = both - fc1_rows
    return pl.pallas_call(
        functools.partial(fc_kernel, fc1_rows, grps),
        grid=(lines,),
        in_specs=[pl.BlockSpec((1, 4, both, cols), lambda i: (i, 0, 0, 0))],
        out_specs=[
            pl.BlockSpec((1, fc1_rows, 4 * cols), lambda i: (i, 0, 0)),
            pl.BlockSpec((4, 1, fc2_rows, cols), lambda i: (0, i, 0, 0)),
        ],
        out_shape=[
            jax.ShapeDtypeStruct((lines, fc1_rows, 4 * cols), F32),
            jax.ShapeDtypeStruct((4, lines, fc2_rows, cols), F32),
        ],
        cost_estimate=pl.CostEstimate(
            flops=0, bytes_accessed=24 * lines * both * cols, transcendentals=0
        ),
        name="place_fc",
    )(x)


def take_heads_kernel(pair, place_ref, x_ref, out_ref):
    grp = place_ref[1]
    width = x_ref.shape[2] // 3
    rows = width // pair // 2
    for unit in range(pair):
        index = lax.rem(grp - unit + pair * 2, pair)
        for core in range(2):
            for kind in range(3):
                start = kind * width + (2 * unit + core) * rows
                out_ref[index, core, :, kind * rows : (kind + 1) * rows] = x_ref[0, :, start : start + rows]


def heads_for(x, core, grp, chip):
    _, share, cols = x.shape
    grps = lax.axis_size("grp")
    rows = cols // 3 // grps
    return pl.pallas_call(
        functools.partial(take_heads_kernel, grps // 2),
        grid_spec=pltpu.PrefetchScalarGridSpec(
            num_scalar_prefetch=1,
            grid=(1,),
            in_specs=[pl.BlockSpec((1, share, cols), lambda i, table: (table[2], 0, 0))],
            out_specs=pl.BlockSpec((grps // 2, 2, share, 3 * rows), lambda i, table: (0, 0, 0, 0)),
        ),
        out_shape=jax.ShapeDtypeStruct((grps // 2, 2, share, 3 * rows), BF),
        cost_estimate=pl.CostEstimate(flops=0, bytes_accessed=4 * share * cols, transcendentals=0),
        name="take_heads",
    )(jnp.stack([core, grp, chip]).astype(jnp.int32), x)


def layer_norm(values):
    centre = values - jnp.mean(values, axis=-1, keepdims=True)
    inverse = lax.rsqrt(jnp.mean(centre * centre, axis=-1, keepdims=True) + EPS)
    return (centre * inverse, inverse)


def norm_back(normed, inverse, grad):
    return inverse * (
        grad
        - jnp.mean(grad, axis=-1, keepdims=True)
        - normed * jnp.mean(grad * normed, axis=-1, keepdims=True)
    )


def silu_float(values):
    return values * jax.nn.sigmoid(values)


def gelu_float(values):
    return jax.nn.gelu(values, approximate=True)


def block_step(
    reps,
    grps,
    latents,
    condition,
    cotangent,
    ada_weight,
    ada_bias,
    qkv_weight,
    qv_bias,
    proj_weight,
    proj_bias,
    fc1_weight,
    fc1_bias,
    fc2_weight,
    fc2_bias,
):
    width = latents.shape[2]
    part = latents.shape[1]
    seq = part * grps
    rows = width // grps
    hidden_width = fc1_weight.shape[1]
    chips = reps // 2
    pair = grps // 2
    share = rows // chips
    rep, grp = lax.axis_index("rep"), lax.axis_index("grp")
    chip, core = rep // 2, rep % 2
    quarter = hidden_width // 4
    mesh_axes = ("rep", "grp")
    tile = min(256, seq)
    served = grp // pair
    block = grp % pair * 2 + core
    lines = reps // 4
    line, rank = rep // 4, rep % 4
    fc1_rows, fc2_rows = rows // lines, quarter // grps // lines

    def shift(x, amount):
        return lax.ppermute(x, "grp", [(g, (g + amount) % grps) for g in range(grps)])

    def partner(x):
        return lax.ppermute(x, "rep", [(r, r ^ 1) for r in range(reps)])

    def hop(x, mask):
        return lax.ppermute(x, "rep", [(r, r ^ (2 * mask)) for r in range(reps)])

    def meeting(j):
        found = []
        for q in range(chips):
            for c in range(2):
                for g in range(grps):
                    here = (2 * q + c) * grps + g
                    there = (2 * q + g // pair) * grps + c * pair + (g + j) % pair
                    found.append((here, there))
        return found

    def pull(x, j):
        return lax.ppermute(x, mesh_axes, [(b, a) for a, b in meeting(j)])

    def push(x, j):
        return lax.ppermute(x, mesh_axes, meeting(j))

    rounds = (grp + jnp.arange(pair)) % pair
    order = chip ^ jnp.arange(chips)

    def turn(blocks, amount):
        twice = jnp.concatenate([blocks, blocks], axis=0)
        return lax.dynamic_slice_in_dim(twice, amount % grps, grps, 0)

    def exchange(x, sign):
        return [x if j == 0 else shift(x, sign * j) for j in range(grps)]

    def own(array, index, count):
        return lax.dynamic_slice_in_dim(array, index * count, count, 0)

    def pick(array, index):
        return lax.dynamic_index_in_dim(array, index, 0, False)

    def add(terms):
        return sum(t.astype(F32) for t in terms).astype(BF)

    def spread(x):
        return [x] + [hop(x, m) for m in range(1, chips)]

    def scatter(blocks):
        mine = [lax.dynamic_index_in_dim(blocks, chip ^ m, 1, False) for m in range(chips)]
        return [mine[0]] + [hop(mine[m], m) for m in range(1, chips)]

    def to_owners(pieces):
        return [push(pick(pieces, (grp + j) % pair), j) for j in range(pair)]

    def split3(x):
        high = lax.reduce_precision(x, 8, 7)
        middle = lax.reduce_precision(x - high, 8, 7)
        return jnp.concatenate([high, middle, x - high - middle]).astype(BF)

    def row_major(x):
        return with_layout_constraint(x, Layout(major_to_minor=tuple(range(x.ndim))))

    def total(x):
        return jnp.sum(x, axis=0, keepdims=True)

    def four(x):
        far = hop(x, 1)
        return jnp.concatenate([x, partner(x), far, partner(far)])

    def four_sum(x):
        x = x.astype(BF).reshape(4, part, width)
        far = add([x[2], partner(x[3])])
        near = x[0].astype(F32) + partner(x[1]).astype(F32)
        return near + hop(far, 1).astype(F32), far

    def line_sum(blocks):
        mine = list(lax.optimization_barrier([lax.dynamic_index_in_dim(blocks, line ^ m, 1, False) for m in range(lines)]))
        return [mine[0]] + [hop(mine[m], 2 * m) for m in range(1, lines)]

    def line_spread(x):
        return [hop(x, 2 * m) for m in range(1, lines)]

    def grp_sum(blocks):
        turned = turn(blocks, grp)
        return [turned[j] if j == 0 else shift(turned[j], j) for j in range(grps)]

    def after(x, *others):
        return lax.optimization_barrier((x, others))[0]

    cond_float = condition.astype(F32)
    cond_silu = silu_float(cond_float).astype(BF)
    cond_rows = lax.dynamic_slice_in_dim(cond_silu, grp * rows, rows, 1)
    biases = (ada_bias, qv_bias, proj_bias, fc1_bias, fc2_bias)
    small = jnp.concatenate(
        [dot(cond_rows, ada_weight), jnp.concatenate(biases).astype(F32)[None]], axis=1
    )
    heads = heads_for(qkv_weight.reshape(chips, share, 3 * width), core, grp, chip)
    fc1_mine = take_columns(fc1_weight.reshape(lines, fc1_rows, hidden_width), rank, line, grps)
    fc2_mine = own(fc2_weight, rank * lines + line, fc2_rows)
    small = after(small, heads)
    fc1_mine, fc2_mine = after((fc1_mine, fc2_mine), heads)
    small = jnp.concatenate(exchange(small, -1))
    gathered = turn(small, grps - grp)
    heads = [pull(heads[j], j) for j in range(pair)]
    mine = jnp.stack([push(latents[0], j) for j in range(pair)])
    tokens = jnp.concatenate([mine, partner(mine)]).reshape(seq, width)

    proj_mine = after(own(proj_weight, chip, share), mine, heads, small)
    proj_pulled = [pull(proj_mine, j) for j in range(pair)]
    fc1_all = exchange(fc1_mine, 1)
    fc1_own, fc2_own = line_spread(fc1_mine), line_spread(fc2_mine)
    heads = [jnp.stack([pick(x, core) for x in heads]), jnp.stack([pick(x, 1 - core) for x in heads])]
    heads = jnp.concatenate([heads[0], partner(heads[1])])
    both_pairs = jnp.concatenate([core * pair + rounds, (1 - core) * pair + rounds])
    (qkv_heads,) = place(
        spread(heads),
        [(both_pairs[None, :] * chips + order[:, None]).reshape(-1)],
        [jax.ShapeDtypeStruct((grps * chips, share, 3 * rows), BF)],
    )
    qkv_heads = qkv_heads.reshape(width, 3 * rows)

    parts = []
    start = 6 * width
    for b in biases:
        parts.append(gathered[:, start : start + b.shape[0]])
        start += b.shape[0]
    modulation = jnp.sum(gathered[:, : 6 * width], axis=0) + parts[0].reshape(-1)
    _, scale1, gate1, shift2, scale2, gate2 = [
        modulation[None, section * width : (section + 1) * width] for section in range(6)
    ]
    qv_own = lax.dynamic_index_in_dim(parts[1].reshape(2, grps, rows), block, 1, False)
    proj_bias_whole = parts[2].reshape(1, -1)
    fc1_bias_part = lax.dynamic_index_in_dim(parts[3].reshape(grps, 4, -1), rank, 1, False).reshape(1, -1)
    fc2_bias_whole = parts[4].reshape(1, -1)

    mod1 = modulation[None, : 2 * width]
    mod1 = jnp.where(served == core, mod1, partner(mod1))
    normed_all, _ = layer_norm(tokens.astype(F32))
    adapted_all = (normed_all * (1.0 + mod1[:, width:]) + mod1[:, :width]).astype(BF)
    adapted_all = lax.optimization_barrier(adapted_all)
    qkv_bias = jnp.concatenate([qv_own[:1], jnp.zeros((1, rows), F32), qv_own[1:]], axis=1)
    projected = (dot(adapted_all, qkv_heads) + qkv_bias).astype(BF)
    proj_all = spread(jnp.stack(after(proj_pulled, projected)))
    mixed, lse = attend(projected, tile)

    fc1_all = [fc1_all[0]] + fc1_own + [z for y in after(fc1_all[1:], mixed) for z in [y] + line_spread(y)]
    here, there = mixed[: seq // 2], partner(mixed[seq // 2 :])
    mixed = jnp.stack([jnp.where(core == 0, here, there), jnp.where(core == 0, there, here)])
    mixed = mixed.reshape(2, pair, part, rows)
    mixed = jnp.stack([pull(mixed[:, j], j) for j in range(pair)])
    fc2_all = exchange(after(fc2_mine, mixed), 1)
    twice = jnp.concatenate([mixed, mixed])
    mixed = lax.dynamic_slice_in_dim(twice, (pair - grp % pair) % pair, pair, 0)
    attended = mixed.reshape(grps, part, rows).transpose(1, 0, 2).reshape(part, width)

    by_hop = (rounds[None, :] * chips + order[:, None]).reshape(-1)
    proj_all = after(proj_all, mixed)
    (proj_whole,) = place(
        proj_all + [partner(x) for x in proj_all],
        [jnp.concatenate([core * pair * chips + by_hop, (1 - core) * pair * chips + by_hop])],
        [jax.ShapeDtypeStruct((grps * chips, share, width), BF)],
    )
    proj_whole = proj_whole.reshape(width, width)

    input_float = latents[0].astype(F32)
    grad_out = cotangent[0].astype(F32)
    attn_out = dot(attended, proj_whole) + proj_bias_whole
    middle = input_float + gate1 * attn_out
    normed2, inverse2 = layer_norm(middle)
    adapted2 = (normed2 * (1.0 + scale2) + shift2).astype(BF)
    grad_m = grad_out * gate2
    grad_m_b = grad_m.astype(BF)

    at_grp, at_line = (grp - jnp.arange(grps)) % grps, line ^ jnp.arange(lines)
    fc_rows_of = (at_grp[:, None] * lines + at_line[None, :]).reshape(-1)

    def placed(pieces):
        whole = jax.ShapeDtypeStruct((grps * lines, *pieces[0].shape), BF)
        return place([x[None] for x in pieces], [fc_rows_of], [whole])[0].reshape(-1, pieces[0].shape[1])

    fc1_quarter = placed(fc1_all)
    fc2_all = [fc2_all[0]] + fc2_own + [z for y in after(fc2_all[1:], adapted2) for z in [y] + line_spread(y)]
    grad_m_four = four(grad_m_b)
    adapted_four = four(adapted2)
    hidden = dot(adapted_four, fc1_quarter) + fc1_bias_part
    activated = gelu_float(hidden).astype(BF)
    fc2_quarter = placed(after(fc2_all, activated))
    grad_act = dot(grad_m_four, fc2_quarter, NT)
    grad_h = jax.vjp(gelu_float, hidden)[1](grad_act)[0]
    grad_h_b = grad_h.astype(BF)
    grad_a2, far = four_sum(dot(grad_h_b, fc1_quarter, NT))
    adapted_four, activated, grad_m_four = after((adapted_four, activated, grad_m_four), far)
    grad_fc2 = dot(activated, grad_m_four, TN).astype(BF).reshape(grps, lines, fc2_rows, width)
    grad_fc2 = line_sum(grad_fc2)
    adapted_four = after(adapted_four, grad_fc2[0])
    grad_fc1 = dot(adapted_four, grad_h_b, TN).astype(BF)
    grad_fc1 = grad_fc1.reshape(grps, lines, fc1_rows, quarter)
    grad_fc1 = line_sum(grad_fc1)

    grad_mid = grad_out + norm_back(normed2, inverse2, grad_a2 * (1.0 + scale2))
    grad_att = grad_mid * gate1
    grad_att_b = grad_att.astype(BF)
    grad_o = dot(grad_att_b, proj_whole, NT).astype(BF)
    grad_o = grad_o.reshape(part, pair, 2, rows).transpose(1, 2, 0, 3)
    grad_o = [pick(grad_o, (grp + j) % pair) for j in range(pair)]
    mlp_out = dot(after(activated, grad_o), fc2_quarter)
    grad_fc2 = grp_sum(add(after(grad_fc2, mlp_out)))
    mlp_out, _ = four_sum(mlp_out)
    grad_o = jnp.stack([push(x, j) for j, x in enumerate(grad_o)], axis=1)
    grad_o = jnp.concatenate([pick(grad_o, core), partner(pick(grad_o, 1 - core))]).reshape(seq, rows)

    grad_proj = row_major(dot(attended, after(grad_att_b, grad_o), TN).astype(BF))
    proj_here, proj_there = own(grad_proj, core, width // 2), own(grad_proj, 1 - core, width // 2)
    proj_there = partner(proj_there)
    grad_heads, qv_sums = attend_back(projected, grad_o, lse, tile)
    mlp_out = after(mlp_out, grad_heads) + fc2_bias_whole
    output = middle + gate2 * mlp_out
    grad_fc1 = grp_sum(add(after(grad_fc1, grad_heads)))
    grad_qkv = row_major(dot(adapted_all, grad_heads, TN).astype(BF))
    here, there = own(grad_qkv, core, width // 2), own(grad_qkv, 1 - core, width // 2)
    there = partner(there)
    here, there = [x.reshape(pair, chips, share, 3 * rows) for x in (here, there)]
    grad_qkv = [
        jnp.stack([lax.dynamic_index_in_dim(x, chip ^ m, 1, False) for x in (here, there)], axis=1)
        for m in range(chips)
    ]
    grad_heads = after(grad_heads, grad_qkv)
    grad_proj = add(after([proj_here, proj_there], grad_qkv))
    grad_proj = scatter(grad_proj.reshape(pair, chips, share, width))
    grad_a1 = dot(grad_heads, qkv_heads, NT)
    mod1_sums = jnp.concatenate([total(grad_a1), total(grad_a1 * normed_all)], axis=1)
    grad_a1 = grad_a1.astype(BF)
    grad_a1 = add([grad_a1[: seq // 2], partner(grad_a1[seq // 2 :])]).reshape(pair, part, width)
    grad_a1 = sum(pull(grad_a1[j], j).astype(F32) for j in range(pair))
    fc_sums = jnp.concatenate([add(after(grad_fc1, mod1_sums)), add(after(grad_fc2, mod1_sums))])
    fc_sums = lax.all_gather(fc_sums, "rep", axis=0)
    grad_fc1_out, grad_fc2_out = place_fc(fc_sums.reshape(lines, 4, -1, width), fc1_rows, grps)

    grad_proj = add(to_owners(add(after(grad_proj, mod1_sums))))
    grad_proj = add([grad_proj, partner(grad_proj)])

    normed1, inverse1 = layer_norm(input_float)
    grad_latents = grad_mid + norm_back(normed1, inverse1, grad_a1 * (1.0 + scale1))

    grad_qkv = add([grad_qkv[0]] + [hop(grad_qkv[m], m) for m in range(1, chips)])
    qkv_sent = grad_qkv
    grad_qkv = jnp.stack(to_owners(grad_qkv))
    grad_qkv = add([own(grad_qkv, core, pair // 2), partner(own(grad_qkv, 1 - core, pair // 2))])
    last = jnp.concatenate(
        [
            lax.dynamic_slice_in_dim(grad_proj, core * (width // 2), width // 2, 1),
            grad_qkv.transpose(2, 0, 1, 3).reshape(share, -1),
        ],
        axis=1,
    )
    last = lax.all_gather(last, "rep", axis=0)
    grad_proj_out, grad_qkv_out = place_last(last.reshape(chips, 2, share, -1), grp, pair, width)

    spread_h = lax.dynamic_update_index_in_dim(
        jnp.zeros((grps, 4, quarter // grps), F32), total(grad_h).reshape(grps, -1), rank, 1
    ).reshape(1, -1)
    spread_qv = lax.dynamic_update_index_in_dim(
        jnp.zeros((2, grps, rows), F32), qv_sums[:2], block, 1
    )
    spread_mod1 = lax.dynamic_update_index_in_dim(jnp.zeros((2, 2 * width), F32), mod1_sums, served, 0)
    sums = jnp.concatenate(
        [
            total(grad_mid * attn_out),
            total(grad_a2),
            total(grad_a2 * normed2),
            total(grad_out * mlp_out),
            spread_qv.reshape(1, -1),
            total(grad_att),
            spread_h,
            total(grad_m),
            spread_mod1.reshape(1, -1),
        ],
        axis=1,
    )
    sums = sum(after(exchange(sums, 1), qkv_sent))
    sums = jnp.concatenate([sums, cond_rows.astype(F32)], axis=1)
    other = partner(sums)
    ends = sums.shape[1] - 4 * width - rows, sums.shape[1] - rows
    mod1_sums = (sums + other)[:, ends[0] : ends[1]].reshape(2, 2 * width)

    def pair_up(own_rows, other_rows, upper):
        return jnp.concatenate(
            [jnp.where(upper, other_rows, own_rows), jnp.where(upper, own_rows, other_rows)]
        )

    sums = pair_up(sums, other, core == 1)
    sums = jnp.concatenate([mod1_sums, sums[:, : ends[0]], sums[:, ends[1] :]], axis=1)
    mod_own = lax.dynamic_slice_in_dim(sums, core, 1, 0)[:, : 6 * width]
    for bit in range(1, reps.bit_length() - 1):
        other = hop(sums, 1 << (bit - 1))
        sums = pair_up(sums, other, (rep >> bit) % 2 == 1)
    grad_mod = sums[:, : 6 * width]
    cond_all = sums[:, sums.shape[1] - rows :]
    grad_ada = dot(jnp.concatenate([cond_all.astype(BF)] * 3), split3(grad_mod), TN)
    grad_silu = total(dot(split3(mod_own), ada_weight, NT))
    grad_silu = jnp.concatenate(exchange(grad_silu, -1))
    grad_silu = turn(grad_silu, grps - grp).reshape(1, width)
    grad_condition = jax.vjp(silu_float, cond_float)[1](grad_silu)[0]

    bias_grads = []
    summed = total(sums)[0]
    start = 0
    for b in biases:
        count = b.shape[0]
        bias_grads.append(lax.dynamic_slice_in_dim(summed, start + grp * count, count))
        start += grps * count

    return (
        output[None],
        grad_latents[None],
        grad_condition,
        grad_ada,
        bias_grads[0],
        grad_qkv_out.reshape(rows, 3 * width),
        bias_grads[1],
        grad_proj_out.reshape(rows, width),
        bias_grads[2],
        grad_fc1_out.reshape(rows, hidden_width),
        bias_grads[3],
        grad_fc2_out.reshape(-1, width),
        bias_grads[4],
    )


def solution(mesh):
    tokens, vector, matrix = P("rep", "grp", None), P("grp"), P("grp", None)
    weights = (matrix, vector) * 5
    return jax.shard_map(
        functools.partial(block_step, mesh.shape["rep"], mesh.shape["grp"]),
        mesh=mesh,
        in_specs=(tokens, P("rep", None), tokens) + weights,
        out_specs=(tokens, tokens, P("rep", None)) + weights,
        check_vma=False,
    )
```

```python
import functools
import math

import jax
import jax.numpy as jnp
from jax import lax
from jax.experimental import pallas as pl
from jax.experimental.pallas import tpu as pltpu
from jax.experimental.layout import Layout, with_layout_constraint
from jax.sharding import PartitionSpec as P


HDIM = 72
EPS = 1e-06
LOG2E = math.log2(math.e)
BF = jnp.bfloat16
F32 = jnp.float32
NT = (((1,), (1,)), ((), ()))
NN = (((1,), (0,)), ((), ()))
TN = (((0,), (0,)), ((), ()))


def dot(a, b, dims=NN):
    return lax.dot_general(a, b, dims, preferred_element_type=F32)


def parts_of(ref, rows, h):
    width = ref.shape[1] // 3
    return [ref[rows, k * width + h * HDIM : k * width + (h + 1) * HDIM] for k in range(3)]


def attend_kernel(heads, tile, x_ref, o_ref, lse_ref):
    factor = HDIM**-0.5 * LOG2E
    rows = pl.ds(pl.multiple_of(pl.program_id(0) * tile, tile), tile)
    for h in range(heads):
        queries = parts_of(x_ref, rows, h)[0]
        _, keys, values = parts_of(x_ref, slice(None), h)
        scores = dot(keys, queries, NT)
        top = jnp.max(scores, axis=0, keepdims=True)
        weights = jnp.exp2((scores - top) * factor)
        total = jnp.sum(weights, axis=0, keepdims=True)
        mixed = dot(values, weights.astype(BF), TN)
        o_ref[:, h * HDIM : (h + 1) * HDIM] = (mixed / total).T.astype(BF)
        lse_ref[h : h + 1, :] = top * factor + jnp.log2(total)


def attend(x, tile):
    seq, width = x.shape[0], x.shape[1] // 3
    heads = width // HDIM
    return pl.pallas_call(
        functools.partial(attend_kernel, heads, tile),
        grid=(seq // tile,),
        in_specs=[pl.BlockSpec((seq, 3 * width), lambda i: (0, 0))],
        out_specs=[
            pl.BlockSpec((tile, width), lambda i: (i, 0)),
            pl.BlockSpec((heads, tile), lambda i: (0, i)),
        ],
        out_shape=[
            jax.ShapeDtypeStruct((seq, width), BF),
            jax.ShapeDtypeStruct((heads, seq), F32),
        ],
        cost_estimate=pl.CostEstimate(
            flops=4 * seq * seq * width,
            bytes_accessed=8 * seq * width,
            transcendentals=heads * seq * seq,
        ),
        name="attend",
    )(x)


def attend_back_kernel(heads, tile, x_ref, g_ref, lse_ref, d_ref, sum_ref, dk_acc, dv_acc):
    step = pl.program_id(0)
    scale = HDIM**-0.5
    width = heads * HDIM
    rows = pl.ds(pl.multiple_of(step * tile, tile), tile)

    @pl.when(step == 0)
    def _():
        dk_acc[...] = jnp.zeros_like(dk_acc)
        dv_acc[...] = jnp.zeros_like(dv_acc)
        sum_ref[...] = jnp.zeros_like(sum_ref)

    for h in range(heads):
        cols = slice(h * HDIM, (h + 1) * HDIM)
        queries = parts_of(x_ref, rows, h)[0]
        _, keys, values = parts_of(x_ref, slice(None), h)
        grads = g_ref[:, cols]
        probs = jnp.exp2(dot(keys, queries, NT) * (scale * LOG2E) - lse_ref[h : h + 1, :])
        dprobs = dot(values, grads, NT)
        delta = jnp.sum(probs * dprobs, axis=0, keepdims=True)
        dscores = (probs * (dprobs - delta)).astype(BF)
        dq = (dot(keys, dscores, TN) * scale).T
        d_ref[rows, cols] = dq.astype(BF)
        sum_ref[0:1, cols] += jnp.sum(dq, axis=0, keepdims=True)
        dk_acc[h] += dot(dscores, queries)
        dv_acc[h] += dot(probs.astype(BF), grads)

    @pl.when(step == pl.num_programs(0) - 1)
    def _():
        for h in range(heads):
            start = width + h * HDIM
            d_ref[:, start : start + HDIM] = (dk_acc[h] * scale).astype(BF)
            d_ref[:, width + start : width + start + HDIM] = dv_acc[h].astype(BF)
            sum_ref[1:2, h * HDIM : (h + 1) * HDIM] = jnp.sum(dv_acc[h], axis=0, keepdims=True)


def attend_back(x, grads, lse, tile):
    seq, width = x.shape[0], x.shape[1] // 3
    heads = width // HDIM
    whole = pl.BlockSpec((seq, 3 * width), lambda i: (0, 0))
    return pl.pallas_call(
        functools.partial(attend_back_kernel, heads, tile),
        grid=(seq // tile,),
        in_specs=[
            whole,
            pl.BlockSpec((tile, width), lambda i: (i, 0)),
            pl.BlockSpec((heads, tile), lambda i: (0, i)),
        ],
        out_specs=[whole, pl.BlockSpec((8, width), lambda i: (0, 0))],
        out_shape=[
            jax.ShapeDtypeStruct((seq, 3 * width), BF),
            jax.ShapeDtypeStruct((8, width), F32),
        ],
        scratch_shapes=[pltpu.VMEM((heads, seq, HDIM), F32), pltpu.VMEM((heads, seq, HDIM), F32)],
        cost_estimate=pl.CostEstimate(
            flops=10 * seq * seq * width,
            bytes_accessed=14 * seq * width,
            transcendentals=heads * seq * seq,
        ),
        name="attend_back",
    )(x, grads, lse)


def place_kernel(counts, cuts, table_ref, *refs):
    pieces, outs = refs[: len(counts)], refs[len(counts) :]
    start = 0
    for piece, count in zip(pieces, counts):

        def put(i, carry, piece=piece, start=start):
            for k, ((low, high), out) in enumerate(zip(cuts, outs)):
                cols = piece.shape[2]
                value = piece[i, low:high, :].astype(out.dtype)
                row = table_ref[2 * k, start + i]
                if out.shape[2] == cols:
                    out[row] = value
                else:
                    out[row, :, pl.ds(pl.multiple_of(table_ref[2 * k + 1, start + i] * cols, 128), cols)] = value
            return carry

        lax.fori_loop(0, count, put, 0)
        start += count


def place(pieces, places, outs, cuts=None):
    counts = [piece.shape[0] for piece in pieces]
    places = [p if isinstance(p, tuple) else (p, jnp.zeros_like(p)) for p in places]
    cuts = cuts or [(0, pieces[0].shape[1])]
    whole = pl.BlockSpec(memory_space=pltpu.VMEM)
    size = sum(2 * math.prod(x.shape) for x in pieces)
    return pl.pallas_call(
        functools.partial(place_kernel, counts, cuts),
        in_specs=[pl.BlockSpec(memory_space=pltpu.SMEM)] + [whole] * len(pieces),
        out_specs=[whole] * len(outs),
        out_shape=outs,
        cost_estimate=pl.CostEstimate(flops=0, bytes_accessed=3 * size, transcendentals=0),
        name="place",
    )(jnp.stack([x for p in places for x in p]).astype(jnp.int32), *pieces)


def last_kernel(pair, width, place_ref, x_ref, proj_ref, qkv_ref):
    grp = place_ref[0]
    rows = width // pair // 2
    start = width // 2
    for core in range(2):
        proj_ref[0, :, core * start : (core + 1) * start] = x_ref[0, core, :, :start].astype(F32)
    for block in range(2 * pair):
        index = lax.rem(grp - block // 2 + pair * 2, pair)
        for at, sender in [(a, c) for a in range(pair) for c in range(2)]:
            first = start + (at % (pair // 2) * 2 + (block % 2 ^ sender)) * 3 * rows

            @pl.when((index == at) & (grp // pair == sender))
            def _():
                for kind in range(3):
                    qkv_ref[0, :, kind * width + block * rows : kind * width + (block + 1) * rows] = x_ref[
                        0, at // (pair // 2), :, first + kind * rows : first + (kind + 1) * rows
                    ].astype(F32)


def place_last(x, grp, pair, width):
    chips, _, share, cols = x.shape
    return pl.pallas_call(
        functools.partial(last_kernel, pair, width),
        grid_spec=pltpu.PrefetchScalarGridSpec(
            num_scalar_prefetch=1,
            grid=(chips,),
            in_specs=[pl.BlockSpec((1, 2, share, cols), lambda i, table: (i, 0, 0, 0))],
            out_specs=[
                pl.BlockSpec((1, share, width), lambda i, table: (i, 0, 0)),
                pl.BlockSpec((1, share, 3 * width), lambda i, table: (i, 0, 0)),
            ],
        ),
        out_shape=[
            jax.ShapeDtypeStruct((chips, share, width), F32),
            jax.ShapeDtypeStruct((chips, share, 3 * width), F32),
        ],
        cost_estimate=pl.CostEstimate(
            flops=0, bytes_accessed=24 * chips * share * width, transcendentals=0
        ),
        name="place_last",
    )(jnp.stack([grp]).astype(jnp.int32), x)


def take_columns_kernel(grps, place_ref, x_ref, out_ref):
    cols = out_ref.shape[1] // grps
    for rank in range(4):

        @pl.when(place_ref[0] == rank)
        def _():
            for block in range(grps):
                start = (4 * block + rank) * cols
                out_ref[:, block * cols : (block + 1) * cols] = x_ref[0, :, start : start + cols]


def take_columns(x, rank, line, grps):
    _, share, cols = x.shape
    return pl.pallas_call(
        functools.partial(take_columns_kernel, grps),
        grid_spec=pltpu.PrefetchScalarGridSpec(
            num_scalar_prefetch=1,
            grid=(1,),
            in_specs=[pl.BlockSpec((1, share, cols), lambda i, table: (table[1], 0, 0))],
            out_specs=pl.BlockSpec((share, cols // 4), lambda i, table: (0, 0)),
        ),
        out_shape=jax.ShapeDtypeStruct((share, cols // 4), BF),
        cost_estimate=pl.CostEstimate(flops=0, bytes_accessed=3 * share * cols, transcendentals=0),
        name="take_columns",
    )(jnp.stack([rank, line]).astype(jnp.int32), x)


def fc_kernel(fc1_rows, grps, x_ref, fc1_ref, fc2_ref):
    cols = x_ref.shape[3] // grps
    for rank in range(4):
        for block in range(grps):
            start = (4 * block + rank) * cols
            fc1_ref[0, :, start : start + cols] = x_ref[
                0, rank, :fc1_rows, block * cols : (block + 1) * cols
            ].astype(F32)
        fc2_ref[rank, 0] = x_ref[0, rank, fc1_rows:, :].astype(F32)


def place_fc(x, fc1_rows, grps):
    lines, _, both, cols = x.shape
    fc2_rows = both - fc1_rows
    return pl.pallas_call(
        functools.partial(fc_kernel, fc1_rows, grps),
        grid=(lines,),
        in_specs=[pl.BlockSpec((1, 4, both, cols), lambda i: (i, 0, 0, 0))],
        out_specs=[
            pl.BlockSpec((1, fc1_rows, 4 * cols), lambda i: (i, 0, 0)),
            pl.BlockSpec((4, 1, fc2_rows, cols), lambda i: (0, i, 0, 0)),
        ],
        out_shape=[
            jax.ShapeDtypeStruct((lines, fc1_rows, 4 * cols), F32),
            jax.ShapeDtypeStruct((4, lines, fc2_rows, cols), F32),
        ],
        cost_estimate=pl.CostEstimate(
            flops=0, bytes_accessed=24 * lines * both * cols, transcendentals=0
        ),
        name="place_fc",
    )(x)


def take_heads_kernel(pair, place_ref, x_ref, *out_refs):
    grp = place_ref[1]
    width = x_ref.shape[2] // 3
    rows = width // pair // 2
    for j, out_ref in enumerate(out_refs):
        for unit in range(pair):

            @pl.when(lax.rem(grp - j + pair * 2, pair) == unit)
            def _():
                for core in range(2):
                    for kind in range(3):
                        start = kind * width + (2 * unit + core) * rows
                        out_ref[core, :, kind * rows : (kind + 1) * rows] = x_ref[0, :, start : start + rows]


def heads_for(x, core, grp, chip):
    _, share, cols = x.shape
    grps = lax.axis_size("grp")
    rows = cols // 3 // grps
    piece = jax.ShapeDtypeStruct((2, share, 3 * rows), BF)
    return pl.pallas_call(
        functools.partial(take_heads_kernel, grps // 2),
        grid_spec=pltpu.PrefetchScalarGridSpec(
            num_scalar_prefetch=1,
            grid=(1,),
            in_specs=[pl.BlockSpec((1, share, cols), lambda i, table: (table[2], 0, 0))],
            out_specs=[pl.BlockSpec(piece.shape, lambda i, table: (0, 0, 0))] * (grps // 2),
        ),
        out_shape=[piece] * (grps // 2),
        cost_estimate=pl.CostEstimate(flops=0, bytes_accessed=4 * share * cols, transcendentals=0),
        name="take_heads",
    )(jnp.stack([core, grp, chip]).astype(jnp.int32), x)


def layer_norm(values):
    centre = values - jnp.mean(values, axis=-1, keepdims=True)
    inverse = lax.rsqrt(jnp.mean(centre * centre, axis=-1, keepdims=True) + EPS)
    return (centre * inverse, inverse)


def norm_back(normed, inverse, grad):
    return inverse * (
        grad
        - jnp.mean(grad, axis=-1, keepdims=True)
        - normed * jnp.mean(grad * normed, axis=-1, keepdims=True)
    )


def silu_float(values):
    return values * jax.nn.sigmoid(values)


def gelu_float(values):
    return jax.nn.gelu(values, approximate=True)


def block_step(
    reps,
    grps,
    latents,
    condition,
    cotangent,
    ada_weight,
    ada_bias,
    qkv_weight,
    qv_bias,
    proj_weight,
    proj_bias,
    fc1_weight,
    fc1_bias,
    fc2_weight,
    fc2_bias,
):
    width = latents.shape[2]
    part = latents.shape[1]
    seq = part * grps
    rows = width // grps
    hidden_width = fc1_weight.shape[1]
    chips = reps // 2
    pair = grps // 2
    share = rows // chips
    rep, grp = lax.axis_index("rep"), lax.axis_index("grp")
    chip, core = rep // 2, rep % 2
    quarter = hidden_width // 4
    mesh_axes = ("rep", "grp")
    tile = min(512, seq)
    served = grp // pair
    block = grp % pair * 2 + core
    lines = reps // 4
    line, rank = rep // 4, rep % 4
    fc1_rows, fc2_rows = rows // lines, quarter // grps // lines

    def shift(x, amount):
        return lax.ppermute(x, "grp", [(g, (g + amount) % grps) for g in range(grps)])

    def partner(x):
        return lax.ppermute(x, "rep", [(r, r ^ 1) for r in range(reps)])

    def hop(x, mask):
        return lax.ppermute(x, "rep", [(r, r ^ (2 * mask)) for r in range(reps)])

    def meeting(j):
        found = []
        for q in range(chips):
            for c in range(2):
                for g in range(grps):
                    here = (2 * q + c) * grps + g
                    there = (2 * q + g // pair) * grps + c * pair + (g + j) % pair
                    found.append((here, there))
        return found

    def pull(x, j):
        return lax.ppermute(x, mesh_axes, [(b, a) for a, b in meeting(j)])

    def push(x, j):
        return lax.ppermute(x, mesh_axes, meeting(j))

    rounds = (grp + jnp.arange(pair)) % pair
    order = chip ^ jnp.arange(chips)

    def turn(blocks, amount):
        twice = jnp.concatenate([blocks, blocks], axis=0)
        return lax.dynamic_slice_in_dim(twice, amount % grps, grps, 0)

    def exchange(x, sign):
        return [x if j == 0 else shift(x, sign * j) for j in range(grps)]

    def own(array, index, count):
        return lax.dynamic_slice_in_dim(array, index * count, count, 0)

    def pick(array, index):
        return lax.dynamic_index_in_dim(array, index, 0, False)

    def add(terms):
        return sum(t.astype(F32) for t in terms).astype(BF)

    def spread(x):
        return [x] + [hop(x, m) for m in range(1, chips)]

    def scatter(blocks):
        mine = [lax.dynamic_index_in_dim(blocks, chip ^ m, 1, False) for m in range(chips)]
        return [mine[0]] + [hop(mine[m], m) for m in range(1, chips)]

    def to_owners(pieces):
        return [push(pick(pieces, (grp + j) % pair), j) for j in range(pair)]

    def split3(x):
        high = lax.reduce_precision(x, 8, 7)
        middle = lax.reduce_precision(x - high, 8, 7)
        return jnp.concatenate([high, middle, x - high - middle]).astype(BF)

    def row_major(x):
        return with_layout_constraint(x, Layout(major_to_minor=tuple(range(x.ndim))))

    def total(x):
        return jnp.sum(x, axis=0, keepdims=True)

    def four(x):
        far = hop(x, 1)
        return jnp.concatenate([x, partner(x), far, partner(far)])

    def four_sum(x):
        x = x.astype(BF).reshape(4, part, width)
        far = add([x[2], partner(x[3])])
        near = x[0].astype(F32) + partner(x[1]).astype(F32)
        return near + hop(far, 1).astype(F32), far

    def line_sum(blocks):
        mine = list(lax.optimization_barrier([lax.dynamic_index_in_dim(blocks, line ^ m, 1, False) for m in range(lines)]))
        return [mine[0]] + [hop(mine[m], 2 * m) for m in range(1, lines)]

    def line_spread(x):
        return [hop(x, 2 * m) for m in range(1, lines)]

    def grp_sum(blocks):
        turned = turn(blocks, grp)
        return [turned[j] if j == 0 else shift(turned[j], j) for j in range(grps)]

    def after(x, *others):
        return lax.optimization_barrier((x, others))[0]

    cond_float = condition.astype(F32)
    cond_silu = silu_float(cond_float).astype(BF)
    cond_rows = lax.dynamic_slice_in_dim(cond_silu, grp * rows, rows, 1)
    biases = (ada_bias, qv_bias, proj_bias, fc1_bias, fc2_bias)
    small = jnp.concatenate(
        [dot(cond_rows, ada_weight), jnp.concatenate(biases).astype(F32)[None]], axis=1
    )
    heads = heads_for(qkv_weight.reshape(chips, share, 3 * width), core, grp, chip)
    fc1_mine = take_columns(fc1_weight.reshape(lines, fc1_rows, hidden_width), rank, line, grps)
    fc2_mine = own(fc2_weight, rank * lines + line, fc2_rows)
    small = after(small, heads)
    fc1_mine, fc2_mine = after((fc1_mine, fc2_mine), heads)
    small = jnp.concatenate(exchange(small, -1))
    gathered = turn(small, grps - grp)
    heads = [pull(heads[j], j) for j in range(pair)]
    mine = jnp.stack([push(latents[0], j) for j in range(pair)])
    tokens = jnp.concatenate([mine, partner(mine)]).reshape(seq, width)

    proj_mine = after(own(proj_weight, chip, share), mine, heads, small)
    proj_pulled = [pull(proj_mine, j) for j in range(pair)]
    fc1_all = exchange(fc1_mine, 1)
    fc1_own, fc2_own = line_spread(fc1_mine), line_spread(fc2_mine)
    heads = [jnp.stack([pick(x, core) for x in heads]), jnp.stack([pick(x, 1 - core) for x in heads])]
    heads = jnp.concatenate([heads[0], partner(heads[1])])
    both_pairs = jnp.concatenate([core * pair + rounds, (1 - core) * pair + rounds])
    (qkv_heads,) = place(
        spread(heads),
        [(both_pairs[None, :] * chips + order[:, None]).reshape(-1)],
        [jax.ShapeDtypeStruct((grps * chips, share, 3 * rows), BF)],
    )
    qkv_heads = qkv_heads.reshape(width, 3 * rows)

    parts = []
    start = 6 * width
    for b in biases:
        parts.append(gathered[:, start : start + b.shape[0]])
        start += b.shape[0]
    modulation = jnp.sum(gathered[:, : 6 * width], axis=0) + parts[0].reshape(-1)
    _, scale1, gate1, shift2, scale2, gate2 = [
        modulation[None, section * width : (section + 1) * width] for section in range(6)
    ]
    qv_own = lax.dynamic_index_in_dim(parts[1].reshape(2, grps, rows), block, 1, False)
    proj_bias_whole = parts[2].reshape(1, -1)
    fc1_bias_part = lax.dynamic_index_in_dim(parts[3].reshape(grps, 4, -1), rank, 1, False).reshape(1, -1)
    fc2_bias_whole = parts[4].reshape(1, -1)

    mod1 = modulation[None, : 2 * width]
    mod1 = jnp.where(served == core, mod1, partner(mod1))
    normed_all, _ = layer_norm(tokens.astype(F32))
    adapted_all = (normed_all * (1.0 + mod1[:, width:]) + mod1[:, :width]).astype(BF)
    adapted_all = lax.optimization_barrier(adapted_all)
    qkv_bias = jnp.concatenate([qv_own[:1], jnp.zeros((1, rows), F32), qv_own[1:]], axis=1)
    projected = (dot(adapted_all, qkv_heads) + qkv_bias).astype(BF)
    proj_all = spread(jnp.stack(after(proj_pulled, qkv_heads)))
    mixed, lse = attend(projected, tile)

    fc1_all = [fc1_all[0]] + fc1_own + [z for y in after(fc1_all[1:], mixed) for z in [y] + line_spread(y)]
    here, there = mixed[: seq // 2], partner(mixed[seq // 2 :])
    mixed = jnp.stack([jnp.where(core == 0, here, there), jnp.where(core == 0, there, here)])
    mixed = mixed.reshape(2, pair, part, rows)
    mixed = jnp.stack([pull(mixed[:, j], j) for j in range(pair)])
    fc2_all = exchange(after(fc2_mine, mixed), 1)
    twice = jnp.concatenate([mixed, mixed])
    mixed = lax.dynamic_slice_in_dim(twice, (pair - grp % pair) % pair, pair, 0)
    attended = mixed.reshape(grps, part, rows).transpose(1, 0, 2).reshape(part, width)

    by_hop = (rounds[None, :] * chips + order[:, None]).reshape(-1)
    (proj_whole,) = place(
        proj_all + [partner(x) for x in proj_all],
        [jnp.concatenate([core * pair * chips + by_hop, (1 - core) * pair * chips + by_hop])],
        [jax.ShapeDtypeStruct((grps * chips, share, width), BF)],
    )
    proj_whole = proj_whole.reshape(width, width)

    input_float = latents[0].astype(F32)
    grad_out = cotangent[0].astype(F32)
    attn_out = dot(attended, proj_whole) + proj_bias_whole
    middle = input_float + gate1 * attn_out
    normed2, inverse2 = layer_norm(middle)
    adapted2 = (normed2 * (1.0 + scale2) + shift2).astype(BF)
    grad_m = grad_out * gate2
    grad_m_b = grad_m.astype(BF)

    at_grp, at_line = (grp - jnp.arange(grps)) % grps, line ^ jnp.arange(lines)
    fc_rows_of = (at_grp[:, None] * lines + at_line[None, :]).reshape(-1)

    def placed(pieces):
        whole = jax.ShapeDtypeStruct((grps * lines, *pieces[0].shape), BF)
        return place([x[None] for x in pieces], [fc_rows_of], [whole])[0].reshape(-1, pieces[0].shape[1])

    fc1_quarter = placed(fc1_all)
    fc2_all = [fc2_all[0]] + fc2_own + [z for y in after(fc2_all[1:], adapted2) for z in [y] + line_spread(y)]
    grad_m_four = lax.optimization_barrier(four(grad_m_b))
    adapted_four = four(adapted2)
    hidden = dot(adapted_four, fc1_quarter) + fc1_bias_part
    activated = gelu_float(hidden).astype(BF)
    fc2_quarter = placed(after(fc2_all, activated))
    grad_act = dot(grad_m_four, fc2_quarter, NT)
    grad_h = jax.vjp(gelu_float, hidden)[1](grad_act)[0]
    grad_h_b = grad_h.astype(BF)
    grad_a2, far = four_sum(dot(grad_h_b, fc1_quarter, NT))
    adapted_four, activated, grad_m_four = after((adapted_four, activated, grad_m_four), far)
    grad_fc2 = dot(activated, grad_m_four, TN).astype(BF).reshape(grps, lines, fc2_rows, width)
    grad_fc2 = line_sum(grad_fc2)
    adapted_four = after(adapted_four, grad_fc2[0])
    grad_fc1 = dot(adapted_four, grad_h_b, TN).astype(BF)
    grad_fc1 = grad_fc1.reshape(grps, lines, fc1_rows, quarter)
    grad_fc1 = line_sum(grad_fc1)

    grad_mid = grad_out + norm_back(normed2, inverse2, grad_a2 * (1.0 + scale2))
    grad_att = grad_mid * gate1
    grad_att_b = grad_att.astype(BF)
    grad_o = dot(grad_att_b, proj_whole, NT).astype(BF)
    grad_o = grad_o.reshape(part, pair, 2, rows).transpose(1, 2, 0, 3)
    grad_o = [pick(grad_o, (grp + j) % pair) for j in range(pair)]
    mlp_out = dot(after(activated, grad_o), fc2_quarter)
    grad_fc2 = grp_sum(add(after(grad_fc2, mlp_out)))
    mlp_out, _ = four_sum(mlp_out)
    grad_o = jnp.stack([push(x, j) for j, x in enumerate(grad_o)], axis=1)
    grad_o = jnp.concatenate([pick(grad_o, core), partner(pick(grad_o, 1 - core))]).reshape(seq, rows)

    grad_proj = row_major(dot(attended, after(grad_att_b, grad_o), TN).astype(BF))
    proj_here, proj_there = own(grad_proj, core, width // 2), own(grad_proj, 1 - core, width // 2)
    proj_there = partner(proj_there)
    grad_proj = add([proj_here, proj_there])
    grad_proj = scatter(grad_proj.reshape(pair, chips, share, width))
    grad_heads, qv_sums = attend_back(projected, grad_o, lse, tile)
    mlp_out = after(mlp_out, grad_heads) + fc2_bias_whole
    output = middle + gate2 * mlp_out
    grad_fc1 = grp_sum(add(after(grad_fc1, grad_heads)))
    grad_qkv = row_major(dot(adapted_all, grad_heads, TN).astype(BF))
    here, there = own(grad_qkv, core, width // 2), own(grad_qkv, 1 - core, width // 2)
    there = partner(there)
    here, there = [x.reshape(pair, chips, share, 3 * rows) for x in (here, there)]
    grad_qkv = [
        jnp.stack([lax.dynamic_index_in_dim(x, chip ^ m, 1, False) for x in (here, there)], axis=1)
        for m in range(chips)
    ]
    grad_heads = after(grad_heads, grad_qkv)
    grad_a1 = dot(grad_heads, qkv_heads, NT)
    mod1_sums = jnp.concatenate([total(grad_a1), total(grad_a1 * normed_all)], axis=1)
    grad_a1 = grad_a1.astype(BF)
    grad_a1 = add([grad_a1[: seq // 2], partner(grad_a1[seq // 2 :])]).reshape(pair, part, width)
    grad_a1 = sum(pull(grad_a1[j], j).astype(F32) for j in range(pair))
    fc_sums = jnp.concatenate([add(after(grad_fc1, mod1_sums)), add(after(grad_fc2, mod1_sums))])
    fc_sums = lax.all_gather(fc_sums, "rep", axis=0)
    grad_fc1_out, grad_fc2_out = place_fc(fc_sums.reshape(lines, 4, -1, width), fc1_rows, grps)

    grad_proj = add(to_owners(add(after(grad_proj, grad_heads))))
    grad_proj = add([grad_proj, partner(grad_proj)])

    normed1, inverse1 = layer_norm(input_float)
    grad_latents = grad_mid + norm_back(normed1, inverse1, grad_a1 * (1.0 + scale1))

    grad_qkv = add([grad_qkv[0]] + [hop(grad_qkv[m], m) for m in range(1, chips)])
    qkv_sent = grad_qkv
    grad_qkv = jnp.stack(to_owners(grad_qkv))
    grad_qkv = add([own(grad_qkv, core, pair // 2), partner(own(grad_qkv, 1 - core, pair // 2))])
    last = jnp.concatenate(
        [
            lax.dynamic_slice_in_dim(grad_proj, core * (width // 2), width // 2, 1),
            grad_qkv.transpose(2, 0, 1, 3).reshape(share, -1),
        ],
        axis=1,
    )
    last = lax.all_gather(last, "rep", axis=0)
    grad_proj_out, grad_qkv_out = place_last(last.reshape(chips, 2, share, -1), grp, pair, width)

    spread_h = lax.dynamic_update_index_in_dim(
        jnp.zeros((grps, 4, quarter // grps), F32), total(grad_h).reshape(grps, -1), rank, 1
    ).reshape(1, -1)
    spread_qv = lax.dynamic_update_index_in_dim(
        jnp.zeros((2, grps, rows), F32), qv_sums[:2], block, 1
    )
    spread_mod1 = lax.dynamic_update_index_in_dim(jnp.zeros((2, 2 * width), F32), mod1_sums, served, 0)
    sums = jnp.concatenate(
        [
            total(grad_mid * attn_out),
            total(grad_a2),
            total(grad_a2 * normed2),
            total(grad_out * mlp_out),
            spread_qv.reshape(1, -1),
            total(grad_att),
            spread_h,
            total(grad_m),
            spread_mod1.reshape(1, -1),
        ],
        axis=1,
    )
    sums = sum(after(exchange(sums, 1), qkv_sent))
    sums = jnp.concatenate([sums, cond_rows.astype(F32)], axis=1)
    other = partner(sums)
    ends = sums.shape[1] - 4 * width - rows, sums.shape[1] - rows
    mod1_sums = (sums + other)[:, ends[0] : ends[1]].reshape(2, 2 * width)

    def pair_up(own_rows, other_rows, upper):
        return jnp.concatenate(
            [jnp.where(upper, other_rows, own_rows), jnp.where(upper, own_rows, other_rows)]
        )

    sums = pair_up(sums, other, core == 1)
    sums = jnp.concatenate([mod1_sums, sums[:, : ends[0]], sums[:, ends[1] :]], axis=1)
    mod_own = lax.dynamic_slice_in_dim(sums, core, 1, 0)[:, : 6 * width]
    for bit in range(1, reps.bit_length() - 1):
        other = hop(sums, 1 << (bit - 1))
        sums = pair_up(sums, other, (rep >> bit) % 2 == 1)
    grad_mod = sums[:, : 6 * width]
    cond_all = sums[:, sums.shape[1] - rows :]
    grad_ada = dot(jnp.concatenate([cond_all.astype(BF)] * 3), split3(grad_mod), TN)
    grad_silu = total(dot(split3(mod_own), ada_weight, NT))
    grad_silu = jnp.concatenate(exchange(grad_silu, -1))
    grad_silu = turn(grad_silu, grps - grp).reshape(1, width)
    grad_condition = jax.vjp(silu_float, cond_float)[1](grad_silu)[0]

    bias_grads = []
    summed = total(sums)[0]
    start = 0
    for b in biases:
        count = b.shape[0]
        bias_grads.append(lax.dynamic_slice_in_dim(summed, start + grp * count, count))
        start += grps * count

    return (
        output[None],
        grad_latents[None],
        grad_condition,
        grad_ada,
        bias_grads[0],
        grad_qkv_out.reshape(rows, 3 * width),
        bias_grads[1],
        grad_proj_out.reshape(rows, width),
        bias_grads[2],
        grad_fc1_out.reshape(rows, hidden_width),
        bias_grads[3],
        grad_fc2_out.reshape(-1, width),
        bias_grads[4],
    )


def solution(mesh):
    tokens, vector, matrix = P("rep", "grp", None), P("grp"), P("grp", None)
    weights = (matrix, vector) * 5
    return jax.shard_map(
        functools.partial(block_step, mesh.shape["rep"], mesh.shape["grp"]),
        mesh=mesh,
        in_specs=(tokens, P("rep", None), tokens) + weights,
        out_specs=(tokens, tokens, P("rep", None)) + weights,
        check_vma=False,
    )
```
